128 devices in a mesh: row: 16 (over z, y_lo, core), pair: 8 (over y_hi, x).
Axes of the slice: x: 4, y: 4 (y_hi: 2, y_lo: 2; y = y_hi * 2 + y_lo), z: 4, core: 2. Of those that a mesh axis runs over, the one named last changes fastest.
Arguments:
- slab: float32 [4096, 4096], P(('row', 'pair'))
- plan: int32 [2, 16], replicated, may hold values from 0 to 15, as said below
Outputs:
- rotated: float32 [4096, 4096], P(('row', 'pair'))
- sing_vals: float32 [4096], replicated
The draws below stay inside these ranges and needn't reach their ends.
Inputs may be any that keep to these rules, and one draw needn't show every extreme that they name: Each row of plan is a permutation of the block ids; no two blocks form a pair in two rounds, and the two blocks of a pair in round r sit in two different pairs in round r + 1.
All inputs are finite; a program needn't handle non-finite values.
Results may differ from the reference program's by a relative error of at most 0.00017.
Values sent between devices are 32-bit elements; how exact they have to be, the bound alone decides.
A program may use at most 64 MiB of HBM per device.

```python
import math
import jax
import jax.numpy as jnp
from jax import lax

BLK = 256
ROUNDS = 2
NS_STEPS = 4
NCOL = 4096
ROWS = 4096


def draw_slab(key, part):
    k_noise, k_common, k_cols = jax.random.split(jax.random.fold_in(key, 11), 3)
    noise = jax.random.normal(k_noise, (ROWS, NCOL), jnp.float32)
    common = jax.random.normal(k_common, (ROWS, BLK), jnp.float32)
    mixing = 0.5
    col_scale = jnp.exp(jax.random.uniform(k_cols, (1, NCOL), jnp.float32, math.log(0.5), math.log(2.0)))
    shared = jnp.tile(common, (1, NCOL // BLK))
    return ((noise + mixing * shared) * col_scale).astype(jnp.float32)


def draw_plan(key, part):
    k_labels, k_start, k_order = jax.random.split(jax.random.fold_in(key, 7), 3)
    nblocks = NCOL // BLK
    circle = nblocks - 1
    labels = jax.random.permutation(k_labels, nblocks).astype(jnp.int32)
    start = jax.random.randint(k_start, (), 0, circle, dtype=jnp.int32)
    steps_k = jnp.arange(1, nblocks // 2, dtype=jnp.int32)
    result = []
    for rnd in range(ROUNDS):
        turn_t = (start + rnd) % circle
        first = jnp.concatenate([jnp.full((1,), circle, jnp.int32), (turn_t + steps_k) % circle])
        second = jnp.concatenate([jnp.full((1,), 1, jnp.int32) * turn_t, (turn_t - steps_k + circle) % circle])
        order = jax.random.permutation(jax.random.fold_in(k_order, rnd), nblocks // 2)
        slots = jnp.stack([first[order], second[order]], axis=1).reshape(nblocks)
        result.append(labels[slots])
    return jnp.stack(result).astype(jnp.int32)


def setup_inputs(seed: int = 0) -> dict:
    splits = jax.random.split(jax.random.key(seed), 3)
    slab = draw_slab(jax.random.fold_in(splits[2], 71), 0)
    plan = draw_plan(jax.random.fold_in(splits[2], 71), 0)
    return dict(slab=slab, plan=plan)


HIGH = lax.Precision.HIGHEST

def position(order):
    count = order.shape[0]
    slots = jnp.arange(count, dtype=jnp.int32)
    return lax.optimization_barrier(jnp.sum(jnp.where(order[None, :] == slots[:, None], slots[None, :], 0), axis=1)).astype(jnp.int32)

def rotation(gram, width):
    diag_vals = jnp.diagonal(gram)
    coupling = gram[:width, width:] / (diag_vals[:width, None] + diag_vals[None, width:] + 1e-06)
    zero_part = jnp.zeros((width, width), jnp.float32)
    skew = jnp.concatenate([jnp.concatenate([zero_part, coupling], 1), jnp.concatenate([-coupling.T, zero_part], 1)], 0)
    scale_c = jnp.sqrt(1.0 + jnp.sum(coupling * coupling))
    ident = jnp.eye(2 * width, dtype=jnp.float32)
    turn = (ident + skew) / scale_c
    for step in range(NS_STEPS):
        inner = jnp.dot(turn.T, turn, precision=HIGH, preferred_element_type=jnp.float32)
        turn = 0.5 * jnp.dot(turn, 3.0 * ident - inner, precision=HIGH, preferred_element_type=jnp.float32)
    return turn

def reference(slab, plan):
    total_rows = slab.shape[0]
    nblocks = NCOL // BLK
    blocks = slab.reshape(total_rows, nblocks, BLK)
    current = jnp.take(blocks, plan[0], axis=1)
    for rnd in range(ROUNDS):
        if rnd > 0:
            current = jnp.take(current, position(plan[rnd - 1])[plan[rnd]], axis=1)
        pairs = current.reshape(total_rows, nblocks // 2, 2 * BLK).transpose(1, 0, 2)

        def one_pair(matrix):
            gram = jnp.dot(matrix.T, matrix, precision=HIGH, preferred_element_type=jnp.float32)
            return jnp.dot(matrix, rotation(gram, BLK), precision=HIGH, preferred_element_type=jnp.float32)
        pairs = lax.map(one_pair, pairs)
        current = pairs.transpose(1, 0, 2).reshape(total_rows, nblocks, BLK)
    rotated = jnp.take(current, position(plan[ROUNDS - 1]), axis=1).reshape(total_rows, NCOL)
    sing_vals = jnp.sqrt(lax.optimization_barrier(jnp.sum(rotated * rotated, axis=0)) / total_rows)
    return (rotated, sing_vals)
```

```python
import functools

import jax
import jax.numpy as jnp
from jax import lax
from jax.experimental import pallas as pl
from jax.experimental.pallas import tpu as pltpu
from jax.sharding import PartitionSpec as P

NS_STEPS = 4
MESH = pl.DeviceIdType.MESH
LANE = 128
ROWS_BY_ROWS = (((1,), (1,)), ((), ()))
PLAIN = (((1,), (0,)), ((), ()))


def split(x):
    high = x.astype(jnp.bfloat16)
    low = (x - high.astype(jnp.float32)).astype(jnp.bfloat16)
    return high, low


def dot3(a, b, dims=PLAIN):
    (ah, al), (bh, bl) = a, b
    mul = functools.partial(
        lax.dot_general, dimension_numbers=dims, preferred_element_type=jnp.float32
    )
    return mul(ah, bh) + (mul(ah, bl) + mul(al, bh))


def column(tile, first, width):
    turned = tile.T
    return jnp.concatenate(
        [turned[:, first + i : first + i + 1] for i in range(width // LANE)], axis=0
    )


def line(tile, first, width):
    return jnp.concatenate(
        [tile[first + i : first + i + 1, :] for i in range(width // LANE)], axis=1
    )


def kernel(
    total_rows,
    plan_ref,
    slab_ref,
    out_ref,
    vals_ref,
    xin,
    send_f,
    recv_f,
    part,
    gather_p,
    dpart,
    gather_d,
    gram,
    send_b,
    recv_b,
    spart,
    gather_s,
    sfin,
    recv_s,
    in_sem,
    f_send,
    f_recv,
    p_send,
    p_recv,
    d_send,
    d_recv,
    g_send,
    g_recv,
    b_send,
    b_recv,
    s_send,
    s_recv,
    v_send,
    v_recv,
):
    nrow, npair = lax.axis_size("row"), lax.axis_size("pair")
    r, p = lax.axis_index("row"), lax.axis_index("pair")
    nblocks = 2 * npair
    rows, width = xin.shape[1:]
    half = width // LANE
    group = npair * rows

    def row_peer(k):
        return lax.rem(r + k, nrow)

    def pair_peer(k):
        return lax.rem(p + k, npair)

    def to_row(src, dst, ssem, rsem, peer):
        return pltpu.make_async_remote_copy(
            src_ref=src, dst_ref=dst, send_sem=ssem, recv_sem=rsem,
            device_id={"row": peer}, device_id_type=MESH,
        )

    def to_pair(src, dst, ssem, rsem, peer):
        return pltpu.make_async_remote_copy(
            src_ref=src, dst_ref=dst, send_sem=ssem, recv_sem=rsem,
            device_id={"pair": peer}, device_id_type=MESH,
        )

    barrier = pltpu.get_barrier_semaphore()
    for k in range(1, nrow):
        pl.semaphore_signal(
            barrier, inc=1, device_id={"row": row_peer(k)}, device_id_type=MESH
        )
    for k in range(1, npair):
        pl.semaphore_signal(
            barrier, inc=1, device_id={"pair": pair_peer(k)}, device_id_type=MESH
        )
    loads = [
        pltpu.make_async_copy(
            slab_ref.at[:, j * width : (j + 1) * width], xin.at[j], in_sem.at[j]
        )
        for j in range(nblocks)
    ]
    for load in loads:
        load.start()

    def locate(block):
        slot = jnp.int32(0)
        for j in range(nblocks):
            slot = jnp.where(plan_ref[1, j] == block, j, slot)
        return slot

    def origin(edge, side):
        keep = plan_ref[1, 2 * edge + side]
        other = jnp.int32(0)
        sign = jnp.float32(0.0)
        for j in range(0, nblocks, 2):
            first, second = plan_ref[0, j], plan_ref[0, j + 1]
            other = jnp.where(first == keep, second, other)
            sign = jnp.where(first == keep, -1.0, sign)
            other = jnp.where(second == keep, first, other)
            sign = jnp.where(second == keep, 1.0, sign)
        return keep, other, sign

    for load in loads:
        load.wait()
    signs = []
    for side in range(2):
        keep, other, sign = origin(p, side)
        signs.append(sign)
        recv_f[side, p, :, :width] = xin[keep]
        recv_f[side, p, :, width:] = xin[other]
        for k in range(1, npair):
            keep, other, _ = origin(pair_peer(k), side)
            send_f[side, k, :, :width] = xin[keep]
            send_f[side, k, :, width:] = xin[other]
    pl.semaphore_wait(barrier, nrow + npair - 2)

    def forward(side, k):
        peer = pair_peer(k)
        return to_pair(
            send_f.at[side, k], recv_f.at[side, p], f_send.at[side, k],
            f_recv.at[side, p], peer,
        )

    def forward_in(side, k):
        peer = pair_peer(k)
        return to_pair(
            send_f.at[side, k], recv_f.at[side, peer], f_send.at[side, k],
            f_recv.at[side, peer], peer,
        )

    for side in range(2):
        for k in range(1, npair):
            forward(side, k).start()

    def reduce_start(n, first, second):
        sums = jnp.concatenate(
            [
                jnp.sum(first * first, axis=0, keepdims=True),
                jnp.sum(second * second, axis=0, keepdims=True),
            ],
            axis=1,
        )
        for i in range(2 * half):
            dpart[n, i : i + 1, :] = sums[:, i * LANE : (i + 1) * LANE]
        gather_d[n, r] = dpart[n]
        for k in range(1, nrow):
            to_row(
                dpart.at[n], gather_d.at[n, r], d_send.at[n, k], d_recv.at[n, r],
                row_peer(k),
            ).start()
        part[n] = dot3(split(first.T), split(second)).reshape(part.shape[1:])
        gather_p[n, r] = part[n, r]
        for k in range(1, nrow):
            peer = row_peer(k)
            to_row(
                part.at[n, peer], gather_p.at[n, r], p_send.at[n, k], p_recv.at[n, r],
                peer,
            ).start()

    def reduce_middle(n):
        for k in range(1, nrow):
            peer = row_peer(k)
            to_row(
                part.at[n, peer], gather_p.at[n, peer], p_send.at[n, k],
                p_recv.at[n, peer], peer,
            ).wait_recv()
        total = gather_p[n, 0]
        for j in range(1, nrow):
            total = total + gather_p[n, j]
        gram[n, r] = total
        for k in range(1, nrow):
            to_row(
                gram.at[n, r], gram.at[n, r], g_send.at[n, k], g_recv.at[n, r],
                row_peer(k),
            ).start()
        for k in range(1, nrow):
            peer = row_peer(k)
            to_row(
                dpart.at[n], gather_d.at[n, peer], d_send.at[n, k], d_recv.at[n, peer],
                peer,
            ).wait_recv()
        sums = gather_d[n, 0]
        for j in range(1, nrow):
            sums = sums + gather_d[n, j]
        return column(sums, 0, width) + (line(sums, half, width) + 1e-6)

    def coupling(n, denom):
        for k in range(1, nrow):
            peer = row_peer(k)
            to_row(
                gram.at[n, r], gram.at[n, peer], g_send.at[n, k], g_recv.at[n, peer],
                peer,
            ).wait_recv()
        return gram[n].reshape(width, width) / denom

    ident = (
        lax.broadcasted_iota(jnp.int32, (width, width), 0)
        == lax.broadcasted_iota(jnp.int32, (width, width), 1)
    ).astype(jnp.float32)

    def rotate(couple, keep, sign_other):
        other, sign = sign_other
        scale = 1.0 + jnp.sum(couple * couple, keepdims=True)
        inv = 1.0 / scale
        pieces = split(couple)
        inner = (ident + dot3(pieces, pieces, ROWS_BY_ROWS)) * inv
        out = (keep + sign * dot3(split(other), pieces, ROWS_BY_ROWS)) * jnp.sqrt(inv)
        for step in range(NS_STEPS):
            factor = 1.5 * ident - 0.5 * inner
            fs = split(factor)
            out = dot3(split(out), fs)
            if step + 1 < NS_STEPS:
                inner = dot3(split(inner), split(dot3(fs, fs)))
        return out

    for side in range(2):
        for k in range(1, npair):
            forward_in(side, k).wait_recv()
        both = recv_f[side].reshape(group, 2 * width)
        reduce_start(side, both[:, :width], both[:, width:])
    denoms = [reduce_middle(side) for side in range(2)]
    blocks = []
    for side in range(2):
        couple = coupling(side, denoms[side])
        both = recv_f[side].reshape(group, 2 * width)
        blocks.append(rotate(couple, both[:, :width], (both[:, width:], signs[side])))

    reduce_start(2, blocks[0], blocks[1])
    couple = coupling(2, reduce_middle(2))
    finals = [
        rotate(couple, blocks[0], (blocks[1], -1.0)),
        rotate(couple.T, blocks[1], (blocks[0], 1.0)),
    ]
    for side in range(2):
        send_b[:, side] = finals[side].reshape(npair, rows, width)
        sums = jnp.sum(finals[side] * finals[side], axis=0, keepdims=True)
        for i in range(half):
            spart[side * half + i : side * half + i + 1, :] = sums[
                :, i * LANE : (i + 1) * LANE
            ]
    gather_s[r] = spart[...]
    for k in range(1, nrow):
        to_row(
            spart, gather_s.at[r], s_send.at[k], s_recv.at[r], row_peer(k)
        ).start()
    mine = pl.ds(2 * p, 2)
    for k in range(1, npair):
        peer = pair_peer(k)
        to_pair(
            send_b.at[peer], recv_b.at[mine], b_send.at[k], b_recv.at[p], peer
        ).start()
    recv_b[mine] = send_b[p]

    for k in range(1, nrow):
        peer = row_peer(k)
        to_row(
            spart, gather_s.at[peer], s_send.at[k], s_recv.at[peer], peer
        ).wait_recv()
    sums = gather_s[0]
    for j in range(1, nrow):
        sums = sums + gather_s[j]
    vals = jnp.sqrt(sums / total_rows)
    for side in range(2):
        sfin[side, :half, :] = vals[side * half : (side + 1) * half]
    for k in range(1, npair):
        to_pair(
            sfin, recv_s.at[mine], v_send.at[k], v_recv.at[p], pair_peer(k)
        ).start()
    recv_s[mine] = sfin[...]

    for k in range(1, npair):
        peer = pair_peer(k)
        to_pair(
            send_b.at[peer], recv_b.at[pl.ds(2 * peer, 2)], b_send.at[k],
            b_recv.at[peer], peer,
        ).wait_recv()
        to_pair(
            sfin, recv_s.at[pl.ds(2 * peer, 2)], v_send.at[k], v_recv.at[peer], peer
        ).wait_recv()
    for j in range(nblocks):
        slot = locate(j)
        out_ref[:, j * width : (j + 1) * width] = recv_b[slot]
        vals_ref[j * half : (j + 1) * half, :] = recv_s[slot, :half, :]

    for side in range(2):
        for k in range(1, npair):
            forward(side, k).wait_send()
    for n in range(3):
        for k in range(1, nrow):
            peer = row_peer(k)
            to_row(
                dpart.at[n], gather_d.at[n, r], d_send.at[n, k], d_recv.at[n, r], peer
            ).wait_send()
            to_row(
                part.at[n, peer], gather_p.at[n, r], p_send.at[n, k], p_recv.at[n, r],
                peer,
            ).wait_send()
            to_row(
                gram.at[n, r], gram.at[n, r], g_send.at[n, k], g_recv.at[n, r], peer
            ).wait_send()
    for k in range(1, nrow):
        to_row(
            spart, gather_s.at[r], s_send.at[k], s_recv.at[r], row_peer(k)
        ).wait_send()
    for k in range(1, npair):
        peer = pair_peer(k)
        to_pair(
            send_b.at[peer], recv_b.at[mine], b_send.at[k], b_recv.at[p], peer
        ).wait_send()
        to_pair(
            sfin, recv_s.at[mine], v_send.at[k], v_recv.at[p], peer
        ).wait_send()


def solution(mesh):
    nrow, npair = mesh.shape["row"], mesh.shape["pair"]

    def on_device(slab, plan):
        rows, ncols = slab.shape
        nblocks = 2 * npair
        width = ncols // nblocks
        part_rows = width // nrow
        half = width // LANE
        f32 = jnp.float32
        dma = pltpu.SemaphoreType.DMA
        out, vals = pl.pallas_call(
            functools.partial(kernel, rows * nrow * npair),
            out_shape=(
                jax.ShapeDtypeStruct((rows, ncols), f32),
                jax.ShapeDtypeStruct((nblocks * half, LANE), f32),
            ),
            in_specs=[
                pl.BlockSpec(memory_space=pltpu.SMEM),
                pl.BlockSpec(memory_space=pl.ANY),
            ],
            out_specs=(
                pl.BlockSpec(memory_space=pltpu.VMEM),
                pl.BlockSpec(memory_space=pltpu.VMEM),
            ),
            scratch_shapes=[
                pltpu.VMEM((nblocks, rows, width), f32),
                pltpu.VMEM((2, npair, rows, 2 * width), f32),
                pltpu.VMEM((2, npair, rows, 2 * width), f32),
                pltpu.VMEM((3, nrow, part_rows, width), f32),
                pltpu.VMEM((3, nrow, part_rows, width), f32),
                pltpu.VMEM((3, 8, LANE), f32),
                pltpu.VMEM((3, nrow, 8, LANE), f32),
                pltpu.VMEM((3, nrow, part_rows, width), f32),
                pltpu.VMEM((npair, 2, rows, width), f32),
                pltpu.VMEM((nblocks, rows, width), f32),
                pltpu.VMEM((8, LANE), f32),
                pltpu.VMEM((nrow, 8, LANE), f32),
                pltpu.VMEM((2, 8, LANE), f32),
                pltpu.VMEM((nblocks, 8, LANE), f32),
                dma((nblocks,)),
                dma((2, npair)),
                dma((2, npair)),
                dma((3, nrow)),
                dma((3, nrow)),
                dma((3, nrow)),
                dma((3, nrow)),
                dma((3, nrow)),
                dma((3, nrow)),
                dma((npair,)),
                dma((npair,)),
                dma((nrow,)),
                dma((nrow,)),
                dma((npair,)),
                dma((npair,)),
            ],
            compiler_params=pltpu.CompilerParams(
                collective_id=0, has_side_effects=True, vmem_limit_bytes=48 * 2**20
            ),
        )(plan, slab)
        return out, vals.reshape(ncols)

    return jax.shard_map(
        on_device,
        mesh=mesh,
        in_specs=(P(("row", "pair"), None), P()),
        out_specs=(P(("row", "pair"), None), P()),
        check_vma=False,
    )
```

```python
import functools

import jax
import jax.numpy as jnp
from jax import lax
from jax.experimental import pallas as pl
from jax.experimental.pallas import tpu as pltpu
from jax.sharding import PartitionSpec as P

NS_STEPS = 4
MESH = pl.DeviceIdType.MESH
LANE = 128
ROWS_BY_ROWS = (((1,), (1,)), ((), ()))
PLAIN = (((1,), (0,)), ((), ()))


def split(x):
    high = x.astype(jnp.bfloat16)
    low = (x - high.astype(jnp.float32)).astype(jnp.bfloat16)
    return high, low


def dot3(a, b, dims=PLAIN):
    (ah, al), (bh, bl) = a, b
    mul = functools.partial(
        lax.dot_general, dimension_numbers=dims, preferred_element_type=jnp.float32
    )
    return mul(ah, bh) + (mul(ah, bl) + mul(al, bh))


def column(tile, first, width):
    turned = tile.T
    return jnp.concatenate(
        [turned[:, first + i : first + i + 1] for i in range(width // LANE)], axis=0
    )


def line(tile, first, width):
    return jnp.concatenate(
        [tile[first + i : first + i + 1, :] for i in range(width // LANE)], axis=1
    )


def ring_places(r, p, nrow, npair):
    def slot_peer(slot):
        return {"row": r, "pair": slot}

    def rank_peer(rank):
        return {"row": rank, "pair": p}

    return p, r, slot_peer, rank_peer


def torus_places(r, p):
    core, y_lo, z = lax.rem(r, 2), lax.rem(lax.div(r, 2), 2), lax.div(r, 4)
    y_hi, x = lax.div(p, 4), lax.rem(p, 4)
    y = 2 * y_hi + y_lo

    def device(x, y, z, core):
        return {
            "row": (z * 2 + lax.rem(y, 2)) * 2 + core,
            "pair": lax.div(y, 2) * 4 + x,
        }

    turn = lax.rem(x + z + 2 * y_hi, 4)
    y_other = lax.div(lax.rem(y + 3, 4), 2)

    def slot_peer(slot):
        i, b = lax.div(slot, 2), lax.rem(slot, 2)
        x0 = lax.rem(i - z - 2 * y_hi + 8, 4)
        y1 = lax.rem(2 * y_other + 2 - b, 4)
        z1 = lax.rem(i - x - 2 * lax.div(y1, 2) + 8, 4)
        first = core == 0
        return device(
            jnp.where(first, x0, x),
            jnp.where(first, 2 * y_hi + b, y1),
            jnp.where(first, z, z1),
            core,
        )

    def rank_peer(rank):
        far, t = lax.div(rank, 8), lax.rem(lax.div(rank, 2), 4)
        return device(
            t, y_lo + 2 * far, lax.rem(turn - t - 2 * far + 8, 4), lax.rem(rank, 2)
        )

    return 2 * turn + y_lo, (y_hi * 4 + x) * 2 + core, slot_peer, rank_peer


def locate(plan_ref, block, nblocks):
    slot = jnp.int32(0)
    for j in range(nblocks):
        slot = jnp.where(plan_ref[1, j] == block, j, slot)
    return slot


def kernel(
    total_rows,
    plan_hbm,
    slab_ref,
    recv_b,
    recv_s,
    plan_ref,
    xin,
    send_f,
    recv_f,
    part,
    gather_p,
    dpart,
    gather_d,
    gram,
    send_b,
    spart,
    gather_s,
    sfin,
    in_sem,
    f_send,
    f_recv,
    p_send,
    p_recv,
    d_send,
    d_recv,
    g_send,
    g_recv,
    b_send,
    b_recv,
    s_send,
    s_recv,
    v_send,
    v_recv,
):
    nrow, npair = lax.axis_size("row"), lax.axis_size("pair")
    row, pair = lax.axis_index("row"), lax.axis_index("pair")
    nblocks = 2 * npair
    rows, width = xin.shape[1:]
    half = width // LANE
    group = npair * rows
    if (nrow, npair) == (16, 8):
        p, r, slot_peer, rank_peer = torus_places(row, pair)
    else:
        p, r, slot_peer, rank_peer = ring_places(row, pair, nrow, npair)
    slots = [lax.rem(p + k, npair) for k in range(npair)]
    ranks = [lax.rem(r + k, nrow) for k in range(nrow)]
    by_slot = [None] + [slot_peer(slot) for slot in slots[1:]]
    by_rank = [None] + [rank_peer(rank) for rank in ranks[1:]]
    others, peers = pl.ds(0, nrow - 1), pl.ds(0, npair - 1)

    def copy_to(device, src, dst, ssem, rsem):
        return pltpu.make_async_remote_copy(
            src_ref=src, dst_ref=dst, send_sem=ssem, recv_sem=rsem,
            device_id=device, device_id_type=MESH,
        )

    barrier = pltpu.get_barrier_semaphore()
    for device in by_slot[1:] + by_rank[1:]:
        pl.semaphore_signal(barrier, inc=1, device_id=device, device_id_type=MESH)
    plan_load = pltpu.make_async_copy(plan_hbm, plan_ref, in_sem.at[0])
    plan_load.start()
    for j in range(nblocks):
        pltpu.make_async_copy(
            slab_ref.at[:, j * width : (j + 1) * width], xin.at[j], in_sem.at[1]
        ).start()
    plan_load.wait()

    def origin(edge, side):
        keep = plan_ref[1, 2 * edge + side]
        other = jnp.int32(0)
        sign = jnp.float32(0.0)
        for j in range(0, nblocks, 2):
            first, second = plan_ref[0, j], plan_ref[0, j + 1]
            other = jnp.where(first == keep, second, other)
            sign = jnp.where(first == keep, -1.0, sign)
            other = jnp.where(second == keep, first, other)
            sign = jnp.where(second == keep, 1.0, sign)
        return keep, other, sign

    pltpu.make_async_copy(xin, xin, in_sem.at[1]).wait()
    signs = []
    for side in range(2):
        keep, other, sign = origin(p, side)
        signs.append(sign)
        recv_f[side, p, :, :width] = xin[keep]
        recv_f[side, p, :, width:] = xin[other]
        for k in range(1, npair):
            keep, other, _ = origin(slots[k], side)
            send_f[side, k - 1, :, :width] = xin[keep]
            send_f[side, k - 1, :, width:] = xin[other]
    pl.semaphore_wait(barrier, nrow + npair - 2)

    for side in range(2):
        for k in range(1, npair):
            copy_to(
                by_slot[k], send_f.at[side, k - 1], recv_f.at[side, p], f_send,
                f_recv.at[side],
            ).start()

    def wait_recv(ref, sem):
        copy_to(by_rank[1], ref, ref, sem, sem).wait_recv()

    def wait_send(ref, sem):
        copy_to(by_rank[1], ref, ref, sem, sem).wait_send()

    def reduce_start(n, first, second):
        sums = jnp.concatenate(
            [
                jnp.sum(first * first, axis=0, keepdims=True),
                jnp.sum(second * second, axis=0, keepdims=True),
            ],
            axis=1,
        )
        for i in range(2 * half):
            dpart[n, i : i + 1, :] = sums[:, i * LANE : (i + 1) * LANE]
        gather_d[n, r] = dpart[n]
        for k in range(1, nrow):
            copy_to(
                by_rank[k], dpart.at[n], gather_d.at[n, r], d_send, d_recv.at[n]
            ).start()
        part[n] = dot3(split(first.T), split(second)).reshape(part.shape[1:])
        gather_p[n, r] = part[n, r]
        for k in range(1, nrow):
            copy_to(
                by_rank[k], part.at[n, ranks[k]], gather_p.at[n, r], p_send,
                p_recv.at[n],
            ).start()

    def reduce_middle(n):
        wait_recv(gather_p.at[n, others], p_recv.at[n])
        total = gather_p[n, 0]
        for j in range(1, nrow):
            total = total + gather_p[n, j]
        gram[n, r] = total
        for k in range(1, nrow):
            copy_to(
                by_rank[k], gram.at[n, r], gram.at[n, r], g_send, g_recv.at[n]
            ).start()
        wait_recv(gather_d.at[n, others], d_recv.at[n])
        sums = gather_d[n, 0]
        for j in range(1, nrow):
            sums = sums + gather_d[n, j]
        return column(sums, 0, width) + (line(sums, half, width) + 1e-6)

    def coupling(n, denom):
        wait_recv(gram.at[n, others], g_recv.at[n])
        return gram[n].reshape(width, width) / denom

    ident = (
        lax.broadcasted_iota(jnp.int32, (width, width), 0)
        == lax.broadcasted_iota(jnp.int32, (width, width), 1)
    ).astype(jnp.float32)

    def rotate(couple, keep, sign_other):
        other, sign = sign_other
        scale = 1.0 + jnp.sum(couple * couple, keepdims=True)
        inv = 1.0 / scale
        pieces = split(couple)
        inner = (ident + dot3(pieces, pieces, ROWS_BY_ROWS)) * inv
        out = (keep + sign * dot3(split(other), pieces, ROWS_BY_ROWS)) * jnp.sqrt(inv)
        for step in range(NS_STEPS):
            factor = 1.5 * ident - 0.5 * inner
            fs = split(factor)
            out = dot3(split(out), fs)
            if step + 1 < NS_STEPS:
                inner = dot3(split(inner), split(dot3(fs, fs)))
        return out

    for side in range(2):
        wait_recv(recv_f.at[side, peers], f_recv.at[side])
        both = recv_f[side].reshape(group, 2 * width)
        reduce_start(side, both[:, :width], both[:, width:])
    denoms = [reduce_middle(side) for side in range(2)]
    blocks = []
    for side in range(2):
        couple = coupling(side, denoms[side])
        both = recv_f[side].reshape(group, 2 * width)
        blocks.append(rotate(couple, both[:, :width], (both[:, width:], signs[side])))

    reduce_start(2, blocks[0], blocks[1])
    couple = coupling(2, reduce_middle(2))
    finals = [
        rotate(couple, blocks[0], (blocks[1], -1.0)),
        rotate(couple.T, blocks[1], (blocks[0], 1.0)),
    ]
    for side in range(2):
        send_b[:, side] = finals[side].reshape(npair, rows, width)
        sums = jnp.sum(finals[side] * finals[side], axis=0, keepdims=True)
        for i in range(half):
            spart[side * half + i : side * half + i + 1, :] = sums[
                :, i * LANE : (i + 1) * LANE
            ]
    gather_s[r] = spart[...]
    for k in range(1, nrow):
        copy_to(by_rank[k], spart, gather_s.at[r], s_send, s_recv).start()
    mine = pl.ds(2 * p, 2)
    own = pltpu.make_async_copy(send_b.at[p], recv_b.at[mine], in_sem.at[0])
    own.start()
    for k in range(1, npair):
        copy_to(
            by_slot[k], send_b.at[slots[k]], recv_b.at[mine], b_send, b_recv
        ).start()

    wait_recv(gather_s.at[others], s_recv)
    sums = gather_s[0]
    for j in range(1, nrow):
        sums = sums + gather_s[j]
    vals = jnp.sqrt(sums / total_rows)
    for side in range(2):
        sfin[side] = vals[side * half : (side + 1) * half]
    for k in range(1, npair):
        copy_to(by_slot[k], sfin, recv_s.at[mine], v_send, v_recv).start()
    recv_s[mine] = sfin[...]

    own.wait()
    arrived = pl.ds(0, 2 * (npair - 1))
    wait_send(send_f.at[:, peers], f_send)
    wait_send(gather_d.at[:, others], d_send)
    wait_send(gather_p.at[:, others], p_send)
    wait_send(gram.at[:, others], g_send)
    wait_send(gather_s.at[others], s_send)
    wait_send(send_b.at[peers], b_send)
    wait_send(recv_s.at[arrived], v_send)
    wait_recv(recv_b.at[arrived], b_recv)
    wait_recv(recv_s.at[arrived], v_recv)


def place(plan_ref, blocks_ref, vals_in, out_ref, vals_ref, buffer, in_sem, out_sem):
    nblocks, rows, width = blocks_ref.shape
    half = width // LANE
    batch = 4
    slots = [locate(plan_ref, j, nblocks) for j in range(nblocks)]
    loads, stores = [], []
    for j in range(nblocks):
        columns = pl.ds(j * width, width)
        loads.append(
            pltpu.make_async_copy(
                blocks_ref.at[slots[j]], buffer.at[:, columns], in_sem.at[j]
            )
        )
        loads[-1].start()
    for j in range(nblocks):
        vals_ref[j * half : (j + 1) * half, :] = vals_in[slots[j]]
    for j in range(0, nblocks, batch):
        columns = pl.ds(j * width, batch * width)
        for load in loads[j : j + batch]:
            load.wait()
        stores.append(
            pltpu.make_async_copy(
                buffer.at[:, columns], out_ref.at[:, columns], out_sem.at[j // batch]
            )
        )
        stores[-1].start()
    for store in stores:
        store.wait()


def solution(mesh):
    nrow, npair = mesh.shape["row"], mesh.shape["pair"]
    vmem, smem = pltpu.VMEM, pltpu.SMEM
    anywhere = pl.BlockSpec(memory_space=pl.ANY)

    def on_device(slab, plan):
        rows, ncols = slab.shape
        nblocks = 2 * npair
        width = ncols // nblocks
        part_rows = width // nrow
        half = width // LANE
        f32 = jnp.float32
        dma = pltpu.SemaphoreType.DMA
        arrived, arrived_vals = pl.pallas_call(
            functools.partial(kernel, rows * nrow * npair),
            out_shape=(
                jax.ShapeDtypeStruct((nblocks, rows, width), f32),
                jax.ShapeDtypeStruct((nblocks, half, LANE), f32),
            ),
            in_specs=[anywhere, anywhere],
            out_specs=(anywhere, pl.BlockSpec(memory_space=vmem)),
            scratch_shapes=[
                smem(plan.shape, jnp.int32),
                vmem((nblocks, rows, width), f32),
                vmem((2, npair - 1, rows, 2 * width), f32),
                vmem((2, npair, rows, 2 * width), f32),
                vmem((3, nrow, part_rows, width), f32),
                vmem((3, nrow, part_rows, width), f32),
                vmem((3, 2 * half, LANE), f32),
                vmem((3, nrow, 2 * half, LANE), f32),
                vmem((3, nrow, part_rows, width), f32),
                vmem((npair, 2, rows, width), f32),
                vmem((2 * half, LANE), f32),
                vmem((nrow, 2 * half, LANE), f32),
                vmem((2, half, LANE), f32),
                dma((2,)),
                dma,
                dma((2,)),
                dma,
                dma((3,)),
                dma,
                dma((3,)),
                dma,
                dma((3,)),
                dma,
                dma,
                dma,
                dma,
                dma,
                dma,
            ],
            compiler_params=pltpu.CompilerParams(
                collective_id=0, has_side_effects=True, vmem_limit_bytes=67043328
            ),
        )(plan, slab)
        out, vals = pl.pallas_call(
            place,
            out_shape=(
                jax.ShapeDtypeStruct((rows, ncols), f32),
                jax.ShapeDtypeStruct((nblocks * half, LANE), f32),
            ),
            in_specs=[
                pl.BlockSpec(memory_space=smem),
                anywhere,
                pl.BlockSpec(memory_space=vmem),
            ],
            out_specs=(anywhere, pl.BlockSpec(memory_space=vmem)),
            scratch_shapes=[vmem((rows, ncols), f32), dma((nblocks,)), dma((4,))],
            compiler_params=pltpu.CompilerParams(vmem_limit_bytes=67043328),
        )(plan, arrived, arrived_vals)
        return out, vals.reshape(ncols)

    return jax.shard_map(
        on_device,
        mesh=mesh,
        in_specs=(P(("row", "pair"), None), P()),
        out_specs=(P(("row", "pair"), None), P()),
        check_vma=False,
    )
```

```python
import functools

import jax
import jax.numpy as jnp
from jax import lax
from jax.experimental import pallas as pl
from jax.experimental.pallas import tpu as pltpu
from jax.sharding import PartitionSpec as P

NS_STEPS = 4
CHUNKS = 2
MESH = pl.DeviceIdType.MESH
LANE = 128
ROWS_BY_ROWS = (((1,), (1,)), ((), ()))
PLAIN = (((1,), (0,)), ((), ()))


def split(x):
    high = x.astype(jnp.bfloat16)
    low = (x - high.astype(jnp.float32)).astype(jnp.bfloat16)
    return high, low


def dot3(a, b, dims=PLAIN):
    (ah, al), (bh, bl) = a, b
    mul = functools.partial(
        lax.dot_general, dimension_numbers=dims, preferred_element_type=jnp.float32
    )
    return mul(ah, bh) + (mul(ah, bl) + mul(al, bh))


def column(tile, first, width):
    turned = tile.T
    return jnp.concatenate(
        [turned[:, first + i : first + i + 1] for i in range(width // LANE)], axis=0
    )


def line(tile, first, width):
    return jnp.concatenate(
        [tile[first + i : first + i + 1, :] for i in range(width // LANE)], axis=1
    )


def ring_places(r, p, nrow, npair):
    def slot_peer(slot):
        return {"row": r, "pair": slot}

    def rank_peer(rank):
        return {"row": rank, "pair": p}

    return p, r, slot_peer, rank_peer


def torus_places(r, p):
    core, y_lo, z = lax.rem(r, 2), lax.rem(lax.div(r, 2), 2), lax.div(r, 4)
    y_hi, x = lax.div(p, 4), lax.rem(p, 4)
    y = 2 * y_hi + y_lo

    def device(x, y, z, core):
        return {
            "row": (z * 2 + lax.rem(y, 2)) * 2 + core,
            "pair": lax.div(y, 2) * 4 + x,
        }

    turn = lax.rem(x + z + 2 * y_hi, 4)
    y_other = lax.div(lax.rem(y + 3, 4), 2)

    def slot_peer(slot):
        i, b = lax.div(slot, 2), lax.rem(slot, 2)
        x0 = lax.rem(i - z - 2 * y_hi + 8, 4)
        y1 = lax.rem(2 * y_other + 2 - b, 4)
        z1 = lax.rem(i - x - 2 * lax.div(y1, 2) + 8, 4)
        first = core == 0
        return device(
            jnp.where(first, x0, x),
            jnp.where(first, 2 * y_hi + b, y1),
            jnp.where(first, z, z1),
            core,
        )

    def rank_peer(rank):
        far, t = lax.div(rank, 8), lax.rem(lax.div(rank, 2), 4)
        return device(
            t, y_lo + 2 * far, lax.rem(turn - t - 2 * far + 8, 4), lax.rem(rank, 2)
        )

    return 2 * turn + y_lo, (y_hi * 4 + x) * 2 + core, slot_peer, rank_peer


def locate(plan_ref, block, nblocks):
    slot = jnp.int32(0)
    for j in range(nblocks):
        slot = jnp.where(plan_ref[1, j] == block, j, slot)
    return slot


def kernel(
    total_rows,
    plan_hbm,
    slab_ref,
    out_ref,
    vals_ref,
    recv_b,
    recv_s,
    plan_ref,
    xin,
    send_f,
    recv_f,
    part,
    gather_p,
    dpart,
    gather_d,
    gram,
    send_b,
    spart,
    gather_s,
    sfin,
    in_sem,
    f_send,
    f_recv,
    p_send,
    p_recv,
    d_send,
    d_recv,
    g_send,
    g_recv,
    b_send,
    b_recv,
    s_send,
    s_recv,
    v_send,
    v_recv,
):
    nrow, npair = lax.axis_size("row"), lax.axis_size("pair")
    row, pair = lax.axis_index("row"), lax.axis_index("pair")
    nblocks = 2 * npair
    rows, width = xin.shape[1:]
    half = width // LANE
    group = npair * rows
    if (nrow, npair) == (16, 8):
        p, r, slot_peer, rank_peer = torus_places(row, pair)
    else:
        p, r, slot_peer, rank_peer = ring_places(row, pair, nrow, npair)
    slots = [lax.rem(p + k, npair) for k in range(npair)]
    ranks = [lax.rem(r + k, nrow) for k in range(nrow)]
    by_slot = [None] + [slot_peer(slot) for slot in slots[1:]]
    by_rank = [None] + [rank_peer(rank) for rank in ranks[1:]]
    others, peers = pl.ds(0, nrow - 1), pl.ds(0, npair - 1)

    def copy_to(device, src, dst, ssem, rsem):
        return pltpu.make_async_remote_copy(
            src_ref=src, dst_ref=dst, send_sem=ssem, recv_sem=rsem,
            device_id=device, device_id_type=MESH,
        )

    plan_load = pltpu.make_async_copy(plan_hbm, plan_ref, in_sem.at[0])
    plan_load.start()
    barrier = pltpu.get_barrier_semaphore()
    for device in by_slot[1:] + by_rank[1:]:
        pl.semaphore_signal(barrier, inc=1, device_id=device, device_id_type=MESH)
    for j in range(nblocks):
        pltpu.make_async_copy(
            slab_ref.at[:, j * width : (j + 1) * width], xin.at[j], in_sem.at[1]
        ).start()
    plan_load.wait()

    def origin(edge, side):
        keep = plan_ref[1, 2 * edge + side]
        other = jnp.int32(0)
        sign = jnp.float32(0.0)
        for j in range(0, nblocks, 2):
            first, second = plan_ref[0, j], plan_ref[0, j + 1]
            other = jnp.where(first == keep, second, other)
            sign = jnp.where(first == keep, -1.0, sign)
            other = jnp.where(second == keep, first, other)
            sign = jnp.where(second == keep, 1.0, sign)
        return keep, other, sign

    pltpu.make_async_copy(xin, xin, in_sem.at[1]).wait()
    signs = []
    for side in range(2):
        for k in range(1, npair):
            keep, other, _ = origin(slots[k], side)
            send_f[side, k - 1, :, :width] = xin[keep]
            send_f[side, k - 1, :, width:] = xin[other]
        if side == 0:
            pl.semaphore_wait(barrier, nrow + npair - 2)
        for k in range(1, npair):
            copy_to(
                by_slot[k], send_f.at[side, k - 1], recv_f.at[side, p], f_send,
                f_recv.at[side],
            ).start()
    for side in range(2):
        keep, other, sign = origin(p, side)
        signs.append(sign)
        recv_f[side, p, :, :width] = xin[keep]
        recv_f[side, p, :, width:] = xin[other]

    def wait_recv(ref, sem):
        copy_to(by_rank[1], ref, ref, sem, sem).wait_recv()

    def wait_send(ref, sem):
        copy_to(by_rank[1], ref, ref, sem, sem).wait_send()

    def reduce_start(n, first, second):
        part[n] = dot3(split(first.T), split(second)).reshape(part.shape[1:])
        for h in range(CHUNKS):
            for k in range(1, nrow):
                copy_to(
                    by_rank[k], part.at[n, h, ranks[k]], gather_p.at[n, h, r], p_send,
                    p_recv.at[n, h],
                ).start()
        for h in range(CHUNKS):
            gather_p[n, h, r] = part[n, h, r]
        sums = jnp.concatenate(
            [
                jnp.sum(first * first, axis=0, keepdims=True),
                jnp.sum(second * second, axis=0, keepdims=True),
            ],
            axis=1,
        )
        for i in range(2 * half):
            dpart[n, i : i + 1, :] = sums[:, i * LANE : (i + 1) * LANE]
        for k in range(1, nrow):
            copy_to(
                by_rank[k], dpart.at[n], gather_d.at[n, r], d_send, d_recv.at[n]
            ).start()
        gather_d[n, r] = dpart[n]

    def reduce_middle(n):
        for h in range(CHUNKS):
            wait_recv(gather_p.at[n, h, others], p_recv.at[n, h])
            total = gather_p[n, h, 0]
            for j in range(1, nrow):
                total = total + gather_p[n, h, j]
            gram[n, h, r] = total
            for k in range(1, nrow):
                copy_to(
                    by_rank[k], gram.at[n, h, r], gram.at[n, h, r], g_send, g_recv.at[n]
                ).start()
        wait_recv(gather_d.at[n, others], d_recv.at[n])
        sums = gather_d[n, 0]
        for j in range(1, nrow):
            sums = sums + gather_d[n, j]
        return column(sums, 0, width) + (line(sums, half, width) + 1e-6)

    def coupling(n, denom):
        wait_recv(gram.at[n, :, others], g_recv.at[n])
        return gram[n].reshape(width, width) / denom

    ident = (
        lax.broadcasted_iota(jnp.int32, (width, width), 0)
        == lax.broadcasted_iota(jnp.int32, (width, width), 1)
    ).astype(jnp.float32)

    def rotate(items):
        inners, outs = [], []
        for couple, keep, other, sign in items:
            pieces = split(couple)
            scale = 1.0 + jnp.sum(couple * couple, keepdims=True)
            inv = 1.0 / scale
            inners.append((ident + dot3(pieces, pieces, ROWS_BY_ROWS)) * inv)
            mixed = keep + sign * dot3(split(other), pieces, ROWS_BY_ROWS)
            outs.append(mixed * jnp.sqrt(inv))
        for step in range(NS_STEPS):
            factors = [split(1.5 * ident - 0.5 * inner) for inner in inners]
            if step + 1 == NS_STEPS:
                return [dot3(split(out), fs) for out, fs in zip(outs, factors)]
            inners = [dot3(split(inner), fs) for inner, fs in zip(inners, factors)]
            outs = [dot3(split(out), fs) for out, fs in zip(outs, factors)]
            inners = [dot3(split(inner), fs) for inner, fs in zip(inners, factors)]

    for side in range(2):
        wait_recv(recv_f.at[side, peers], f_recv.at[side])
        both = recv_f[side].reshape(group, 2 * width)
        reduce_start(side, both[:, :width], both[:, width:])
    denoms = [reduce_middle(side) for side in range(2)]
    blocks = []
    for side in range(2):
        couple = coupling(side, denoms[side])
        both = recv_f[side].reshape(group, 2 * width)
        blocks += rotate([(couple, both[:, :width], both[:, width:], signs[side])])

    reduce_start(2, blocks[0], blocks[1])
    couple = coupling(2, reduce_middle(2))
    finals = rotate(
        [(couple, *blocks, -1.0), (couple.T, blocks[1], blocks[0], 1.0)]
    )
    for side in range(2):
        sums = jnp.sum(finals[side] * finals[side], axis=0, keepdims=True)
        for i in range(half):
            spart[side * half + i : side * half + i + 1, :] = sums[
                :, i * LANE : (i + 1) * LANE
            ]
    for k in range(1, nrow):
        copy_to(by_rank[k], spart, gather_s.at[r], s_send, s_recv).start()
    gather_s[r] = spart[...]
    for side in range(2):
        send_b[:, side] = finals[side].reshape(npair, rows, width)
    mine = pl.ds(2 * p, 2)
    for k in range(1, npair):
        copy_to(
            by_slot[k], send_b.at[slots[k]], recv_b.at[mine], b_send, b_recv
        ).start()
    recv_b[mine] = send_b[p]

    wait_recv(gather_s.at[others], s_recv)
    sums = gather_s[0]
    for j in range(1, nrow):
        sums = sums + gather_s[j]
    vals = jnp.sqrt(sums / total_rows)
    for side in range(2):
        sfin[side] = vals[side * half : (side + 1) * half]
    for k in range(1, npair):
        copy_to(by_slot[k], sfin, recv_s.at[mine], v_send, v_recv).start()
    recv_s[mine] = sfin[...]

    arrived = pl.ds(0, 2 * (npair - 1))
    wait_send(send_f.at[:, peers], f_send)
    wait_send(gather_d.at[:, others], d_send)
    wait_send(gather_p.at[:, :, others], p_send)
    wait_send(gram.at[:, :, others], g_send)
    wait_send(gather_s.at[others], s_send)
    wait_send(send_b.at[peers], b_send)
    wait_send(recv_s.at[arrived], v_send)
    wait_recv(recv_b.at[arrived], b_recv)
    wait_recv(recv_s.at[arrived], v_recv)
    for j in range(nblocks):
        slot = locate(plan_ref, j, nblocks)
        out_ref[:, j * width : (j + 1) * width] = recv_b[slot]
        vals_ref[j * half : (j + 1) * half, :] = recv_s[slot]


def solution(mesh):
    nrow, npair = mesh.shape["row"], mesh.shape["pair"]
    vmem, smem = pltpu.VMEM, pltpu.SMEM
    anywhere = pl.BlockSpec(memory_space=pl.ANY)

    def on_device(slab, plan):
        rows, ncols = slab.shape
        nblocks = 2 * npair
        width = ncols // nblocks
        part_rows = width // (nrow * CHUNKS)
        half = width // LANE
        f32 = jnp.float32
        dma = pltpu.SemaphoreType.DMA
        out, vals = pl.pallas_call(
            functools.partial(kernel, rows * nrow * npair),
            out_shape=(
                pltpu.VMEM((rows, ncols), f32),
                pltpu.VMEM((nblocks * half, LANE), f32),
            ),
            in_specs=[anywhere, anywhere],
            out_specs=(pl.BlockSpec(memory_space=vmem), pl.BlockSpec(memory_space=vmem)),
            scratch_shapes=[
                vmem((nblocks, rows, width), f32),
                vmem((nblocks, half, LANE), f32),
                smem(plan.shape, jnp.int32),
                vmem((nblocks, rows, width), f32),
                vmem((2, npair - 1, rows, 2 * width), f32),
                vmem((2, npair, rows, 2 * width), f32),
                vmem((3, CHUNKS, nrow, part_rows, width), f32),
                vmem((3, CHUNKS, nrow, part_rows, width), f32),
                vmem((3, 2 * half, LANE), f32),
                vmem((3, nrow, 2 * half, LANE), f32),
                vmem((3, CHUNKS, nrow, part_rows, width), f32),
                vmem((npair, 2, rows, width), f32),
                vmem((2 * half, LANE), f32),
                vmem((nrow, 2 * half, LANE), f32),
                vmem((2, half, LANE), f32),
                dma((2,)),
                dma,
                dma((2,)),
                dma,
                dma((3, CHUNKS)),
                dma,
                dma((3,)),
                dma,
                dma((3,)),
                dma,
                dma,
                dma,
                dma,
                dma,
                dma,
            ],
            compiler_params=pltpu.CompilerParams(
                collective_id=0, has_side_effects=True, vmem_limit_bytes=66000000
            ),
        )(plan, slab)
        return out, vals.reshape(ncols)

    return jax.shard_map(
        on_device,
        mesh=mesh,
        in_specs=(P(("row", "pair"), None), P()),
        out_specs=(P(("row", "pair"), None), P()),
        check_vma=False,
    )
```

```python
import functools

import jax
import jax.numpy as jnp
from jax import lax
from jax.experimental import pallas as pl
from jax.experimental.pallas import tpu as pltpu
from jax.sharding import PartitionSpec as P

NS_STEPS = 4
CHUNKS = 2
MESH = pl.DeviceIdType.MESH
LANE = 128
ROWS_BY_ROWS = (((1,), (1,)), ((), ()))
PLAIN = (((1,), (0,)), ((), ()))


def split(x):
    high = x.astype(jnp.bfloat16)
    low = (x - high.astype(jnp.float32)).astype(jnp.bfloat16)
    return high, low


def dot3(a, b, dims=PLAIN):
    (ah, al), (bh, bl) = a, b
    mul = functools.partial(
        lax.dot_general, dimension_numbers=dims, preferred_element_type=jnp.float32
    )
    return mul(ah, bh) + (mul(ah, bl) + mul(al, bh))


def column(tile, first, width):
    turned = tile.T
    return jnp.concatenate(
        [turned[:, first + i : first + i + 1] for i in range(width // LANE)], axis=0
    )


def line(tile, first, width):
    return jnp.concatenate(
        [tile[first + i : first + i + 1, :] for i in range(width // LANE)], axis=1
    )


def ring_places(r, p, nrow, npair):
    def slot_peer(slot):
        return {"row": r, "pair": slot}

    def rank_peer(rank):
        return {"row": rank, "pair": p}

    return p, r, slot_peer, rank_peer


def torus_places(r, p):
    core, y_lo, z = lax.rem(r, 2), lax.rem(lax.div(r, 2), 2), lax.div(r, 4)
    y_hi, x = lax.div(p, 4), lax.rem(p, 4)
    y = 2 * y_hi + y_lo

    def device(x, y, z, core):
        return {
            "row": (z * 2 + lax.rem(y, 2)) * 2 + core,
            "pair": lax.div(y, 2) * 4 + x,
        }

    inner = y_lo != y_hi

    def slot_peer(slot):
        h, xx = lax.div(slot, 4), lax.rem(slot, 4)
        return device(xx, jnp.where(inner, 1 + h, 3 * h), z, core)

    def rank_peer(m):
        return device(x, 2 * y_hi + lax.rem(lax.div(m, 2), 2), lax.div(m, 4), lax.rem(m, 2))

    return p, r, slot_peer, rank_peer


def locate(plan_ref, block, nblocks):
    slot = jnp.int32(0)
    for j in range(nblocks):
        slot = jnp.where(plan_ref[1, j] == block, j, slot)
    return slot


def kernel(
    total_rows,
    plan_hbm,
    slab_ref,
    out_ref,
    vals_ref,
    recv_b,
    recv_s,
    plan_ref,
    xin,
    send_f,
    recv_f,
    part,
    gather_p,
    dpart,
    gather_d,
    gram,
    send_b,
    spart,
    gather_s,
    sfin,
    in_sem,
    f_send,
    f_recv,
    p_send,
    p_recv,
    d_send,
    d_recv,
    g_send,
    g_recv,
    b_send,
    b_recv,
    s_send,
    s_recv,
    v_send,
    v_recv,
):
    nrow, npair = lax.axis_size("row"), lax.axis_size("pair")
    row, pair = lax.axis_index("row"), lax.axis_index("pair")
    nblocks = 2 * npair
    rows, width = xin.shape[1:]
    half = width // LANE
    group = npair * rows
    if (nrow, npair) == (16, 8):
        p, r, slot_peer, rank_peer = torus_places(row, pair)
    else:
        p, r, slot_peer, rank_peer = ring_places(row, pair, nrow, npair)
    slots = [lax.rem(p + k, npair) for k in range(npair)]
    ranks = [lax.rem(r + k, nrow) for k in range(nrow)]
    by_slot = [None] + [slot_peer(slot) for slot in slots[1:]]
    by_rank = [None] + [rank_peer(rank) for rank in ranks[1:]]
    others, peers = pl.ds(0, nrow - 1), pl.ds(0, npair - 1)

    def copy_to(device, src, dst, ssem, rsem):
        return pltpu.make_async_remote_copy(
            src_ref=src, dst_ref=dst, send_sem=ssem, recv_sem=rsem,
            device_id=device, device_id_type=MESH,
        )

    plan_load = pltpu.make_async_copy(plan_hbm, plan_ref, in_sem.at[0])
    plan_load.start()
    barrier = pltpu.get_barrier_semaphore()
    for device in by_slot[1:] + by_rank[1:]:
        pl.semaphore_signal(barrier, inc=1, device_id=device, device_id_type=MESH)
    for j in range(nblocks):
        pltpu.make_async_copy(
            slab_ref.at[:, j * width : (j + 1) * width], xin.at[j], in_sem.at[1]
        ).start()
    plan_load.wait()

    def origin(edge, side):
        keep = plan_ref[1, 2 * edge + side]
        other = jnp.int32(0)
        sign = jnp.float32(0.0)
        for j in range(0, nblocks, 2):
            first, second = plan_ref[0, j], plan_ref[0, j + 1]
            other = jnp.where(first == keep, second, other)
            sign = jnp.where(first == keep, -1.0, sign)
            other = jnp.where(second == keep, first, other)
            sign = jnp.where(second == keep, 1.0, sign)
        return keep, other, sign

    pltpu.make_async_copy(xin, xin, in_sem.at[1]).wait()
    signs = []
    for side in range(2):
        for k in range(1, npair):
            keep, other, _ = origin(slots[k], side)
            send_f[side, k - 1, :, :width] = xin[keep]
            send_f[side, k - 1, :, width:] = xin[other]
        if side == 0:
            pl.semaphore_wait(barrier, nrow + npair - 2)
        for k in range(1, npair):
            copy_to(
                by_slot[k], send_f.at[side, k - 1], recv_f.at[side, p], f_send,
                f_recv.at[side],
            ).start()
    for side in range(2):
        keep, other, sign = origin(p, side)
        signs.append(sign)
        recv_f[side, p, :, :width] = xin[keep]
        recv_f[side, p, :, width:] = xin[other]

    def wait_recv(ref, sem):
        copy_to(by_rank[1], ref, ref, sem, sem).wait_recv()

    def wait_send(ref, sem):
        copy_to(by_rank[1], ref, ref, sem, sem).wait_send()

    def reduce_start(n, first, second):
        turned, right = first.T, split(second)
        band = width // CHUNKS
        for h in range(CHUNKS):
            left = split(turned[h * band : (h + 1) * band])
            part[n, h] = dot3(left, right).reshape(part.shape[2:])
            for k in range(1, nrow):
                copy_to(
                    by_rank[k], part.at[n, h, ranks[k]], gather_p.at[n, h, r], p_send,
                    p_recv.at[n, h],
                ).start()
        for h in range(CHUNKS):
            gather_p[n, h, r] = part[n, h, r]
        sums = jnp.concatenate(
            [
                jnp.sum(first * first, axis=0, keepdims=True),
                jnp.sum(second * second, axis=0, keepdims=True),
            ],
            axis=1,
        )
        for i in range(2 * half):
            dpart[n, i : i + 1, :] = sums[:, i * LANE : (i + 1) * LANE]
        for k in range(1, nrow):
            copy_to(
                by_rank[k], dpart.at[n], gather_d.at[n, r], d_send, d_recv.at[n]
            ).start()
        gather_d[n, r] = dpart[n]

    def reduce_middle(n):
        for h in range(CHUNKS):
            wait_recv(gather_p.at[n, h, others], p_recv.at[n, h])
            total = gather_p[n, h, 0]
            for j in range(1, nrow):
                total = total + gather_p[n, h, j]
            gram[n, h, r] = total
            for k in range(1, nrow):
                copy_to(
                    by_rank[k], gram.at[n, h, r], gram.at[n, h, r], g_send, g_recv.at[n]
                ).start()
        wait_recv(gather_d.at[n, others], d_recv.at[n])
        sums = gather_d[n, 0]
        for j in range(1, nrow):
            sums = sums + gather_d[n, j]
        return column(sums, 0, width) + (line(sums, half, width) + 1e-6)

    def coupling(n, denom):
        wait_recv(gram.at[n, :, others], g_recv.at[n])
        return gram[n].reshape(width, width) / denom

    ident = (
        lax.broadcasted_iota(jnp.int32, (width, width), 0)
        == lax.broadcasted_iota(jnp.int32, (width, width), 1)
    ).astype(jnp.float32)

    def rotate(items):
        inners, outs = [], []
        for couple, keep, other, sign in items:
            pieces = split(couple)
            scale = 1.0 + jnp.sum(couple * couple, keepdims=True)
            inv = 1.0 / scale
            inners.append((ident + dot3(pieces, pieces, ROWS_BY_ROWS)) * inv)
            mixed = keep + sign * dot3(split(other), pieces, ROWS_BY_ROWS)
            outs.append(mixed * jnp.sqrt(inv))
        for step in range(NS_STEPS):
            factors = [split(1.5 * ident - 0.5 * inner) for inner in inners]
            if step + 1 == NS_STEPS:
                return [
                    functools.partial(dot3, split(out), fs)
                    for out, fs in zip(outs, factors)
                ]
            inners = [dot3(split(inner), fs) for inner, fs in zip(inners, factors)]
            outs = [dot3(split(out), fs) for out, fs in zip(outs, factors)]
            inners = [dot3(split(inner), fs) for inner, fs in zip(inners, factors)]

    for side in range(2):
        wait_recv(recv_f.at[side, peers], f_recv.at[side])
        both = recv_f[side].reshape(group, 2 * width)
        reduce_start(side, both[:, :width], both[:, width:])
    denoms = [reduce_middle(side) for side in range(2)]
    blocks = []
    for side in range(2):
        couple = coupling(side, denoms[side])
        both = recv_f[side].reshape(group, 2 * width)
        (last,) = rotate([(couple, both[:, :width], both[:, width:], signs[side])])
        blocks.append(last())

    reduce_start(2, blocks[0], blocks[1])
    couple = coupling(2, reduce_middle(2))
    lasts = rotate(
        [(couple, *blocks, -1.0), (couple.T, blocks[1], blocks[0], 1.0)]
    )
    for side in range(2):
        final = lasts[side]()
        send_b[side] = final.reshape(npair, rows, width)
        for k in range(1, npair):
            copy_to(
                by_slot[k], send_b.at[side, slots[k]], recv_b.at[2 * p + side], b_send,
                b_recv,
            ).start()
        sums = jnp.sum(final * final, axis=0, keepdims=True)
        for i in range(half):
            spart[side * half + i : side * half + i + 1, :] = sums[
                :, i * LANE : (i + 1) * LANE
            ]
    for k in range(1, nrow):
        copy_to(by_rank[k], spart, gather_s.at[r], s_send, s_recv).start()
    gather_s[r] = spart[...]
    mine = pl.ds(2 * p, 2)
    for side in range(2):
        recv_b[2 * p + side] = send_b[side, p]

    wait_recv(gather_s.at[others], s_recv)
    sums = gather_s[0]
    for j in range(1, nrow):
        sums = sums + gather_s[j]
    vals = jnp.sqrt(sums / total_rows)
    for side in range(2):
        sfin[side] = vals[side * half : (side + 1) * half]
    for k in range(1, npair):
        copy_to(by_slot[k], sfin, recv_s.at[mine], v_send, v_recv).start()
    recv_s[mine] = sfin[...]

    arrived = pl.ds(0, 2 * (npair - 1))
    wait_send(send_f.at[:, peers], f_send)
    wait_send(gather_d.at[:, others], d_send)
    wait_send(gather_p.at[:, :, others], p_send)
    wait_send(gram.at[:, :, others], g_send)
    wait_send(gather_s.at[others], s_send)
    wait_send(send_b.at[:, peers], b_send)
    wait_send(recv_s.at[arrived], v_send)
    wait_recv(recv_b.at[arrived], b_recv)
    wait_recv(recv_s.at[arrived], v_recv)
    for j in range(nblocks):
        slot = locate(plan_ref, j, nblocks)
        out_ref[:, j * width : (j + 1) * width] = recv_b[slot]
        vals_ref[j * half : (j + 1) * half, :] = recv_s[slot]


def solution(mesh):
    nrow, npair = mesh.shape["row"], mesh.shape["pair"]
    vmem, smem = pltpu.VMEM, pltpu.SMEM
    anywhere = pl.BlockSpec(memory_space=pl.ANY)

    def on_device(slab, plan):
        rows, ncols = slab.shape
        nblocks = 2 * npair
        width = ncols // nblocks
        part_rows = width // (nrow * CHUNKS)
        half = width // LANE
        f32 = jnp.float32
        dma = pltpu.SemaphoreType.DMA
        out, vals = pl.pallas_call(
            functools.partial(kernel, rows * nrow * npair),
            out_shape=(
                pltpu.VMEM((rows, ncols), f32),
                pltpu.VMEM((nblocks * half, LANE), f32),
            ),
            in_specs=[anywhere, anywhere],
            out_specs=(pl.BlockSpec(memory_space=vmem), pl.BlockSpec(memory_space=vmem)),
            scratch_shapes=[
                vmem((nblocks, rows, width), f32),
                vmem((nblocks, half, LANE), f32),
                smem(plan.shape, jnp.int32),
                vmem((nblocks, rows, width), f32),
                vmem((2, npair - 1, rows, 2 * width), f32),
                vmem((2, npair, rows, 2 * width), f32),
                vmem((3, CHUNKS, nrow, part_rows, width), f32),
                vmem((3, CHUNKS, nrow, part_rows, width), f32),
                vmem((3, 2 * half, LANE), f32),
                vmem((3, nrow, 2 * half, LANE), f32),
                vmem((3, CHUNKS, nrow, part_rows, width), f32),
                vmem((2, npair, rows, width), f32),
                vmem((2 * half, LANE), f32),
                vmem((nrow, 2 * half, LANE), f32),
                vmem((2, half, LANE), f32),
                dma((2,)),
                dma,
                dma((2,)),
                dma,
                dma((3, CHUNKS)),
                dma,
                dma((3,)),
                dma,
                dma((3,)),
                dma,
                dma,
                dma,
                dma,
                dma,
                dma,
            ],
            compiler_params=pltpu.CompilerParams(
                collective_id=0, has_side_effects=True, vmem_limit_bytes=66000000
            ),
        )(plan, slab)
        return out, vals.reshape(ncols)

    return jax.shard_map(
        on_device,
        mesh=mesh,
        in_specs=(P(("row", "pair"), None), P()),
        out_specs=(P(("row", "pair"), None), P()),
        check_vma=False,
    )
```

```python
import functools

import jax
import jax.numpy as jnp
from jax import lax
from jax.experimental import pallas as pl
from jax.experimental.pallas import tpu as pltpu
from jax.sharding import PartitionSpec as P

NS_STEPS = 4
CHUNKS = 2
MESH = pl.DeviceIdType.MESH
LANE = 128
ROWS_BY_ROWS = (((1,), (1,)), ((), ()))
PLAIN = (((1,), (0,)), ((), ()))


def split(x):
    high = x.astype(jnp.bfloat16)
    low = (x - high.astype(jnp.float32)).astype(jnp.bfloat16)
    return high, low


def dot3(a, b, dims=PLAIN):
    (ah, al), (bh, bl) = a, b
    mul = functools.partial(
        lax.dot_general, dimension_numbers=dims, preferred_element_type=jnp.float32
    )
    return mul(ah, bh) + (mul(ah, bl) + mul(al, bh))


def column(tile, first, width):
    turned = tile.T
    return jnp.concatenate(
        [turned[:, first + i : first + i + 1] for i in range(width // LANE)], axis=0
    )


def line(tile, first, width):
    return jnp.concatenate(
        [tile[first + i : first + i + 1, :] for i in range(width // LANE)], axis=1
    )


def ring_places(r, p, nrow, npair):
    def slot_peer(slot):
        return {"row": r, "pair": slot}

    def rank_peer(rank):
        return {"row": rank, "pair": p}

    return p, r, slot_peer, rank_peer


def torus_places(r, p):
    core, y_lo, z = lax.rem(r, 2), lax.rem(lax.div(r, 2), 2), lax.div(r, 4)
    y_hi, x = lax.div(p, 4), lax.rem(p, 4)
    y = 2 * y_hi + y_lo

    def device(x, y, z, core):
        return {
            "row": (z * 2 + lax.rem(y, 2)) * 2 + core,
            "pair": lax.div(y, 2) * 4 + x,
        }

    inner = y_lo != y_hi

    def slot_peer(slot):
        h, xx = lax.div(slot, 4), lax.rem(slot, 4)
        return device(xx, jnp.where(inner, 1 + h, 3 * h), z, core)

    def rank_peer(m):
        return device(x, 2 * y_hi + lax.rem(lax.div(m, 2), 2), lax.div(m, 4), lax.rem(m, 2))

    return p, r, slot_peer, rank_peer


def locate(plan_ref, block, nblocks):
    slot = jnp.int32(0)
    for j in range(nblocks):
        slot = jnp.where(plan_ref[1, j] == block, j, slot)
    return slot


def kernel(
    total_rows,
    plan_hbm,
    slab_ref,
    out_ref,
    vals_ref,
    recv_b,
    recv_s,
    plan_ref,
    xin,
    send_f,
    recv_f,
    part,
    gather_p,
    dpart,
    gather_d,
    gram,
    send_b,
    spart,
    gather_s,
    sfin,
    in_sem,
    f_send,
    f_recv,
    p_send,
    p_recv,
    d_send,
    d_recv,
    g_send,
    g_recv,
    b_send,
    b_recv,
    s_send,
    s_recv,
    v_send,
    v_recv,
):
    nrow, npair = lax.axis_size("row"), lax.axis_size("pair")
    row, pair = lax.axis_index("row"), lax.axis_index("pair")
    nblocks = 2 * npair
    rows, width = xin.shape[1:]
    half = width // LANE
    group = npair * rows
    if (nrow, npair) == (16, 8):
        p, r, slot_peer, rank_peer = torus_places(row, pair)
    else:
        p, r, slot_peer, rank_peer = ring_places(row, pair, nrow, npair)
    slots = [lax.rem(p + k, npair) for k in range(npair)]
    ranks = [lax.rem(r + k, nrow) for k in range(nrow)]
    by_slot = [None] + [slot_peer(slot) for slot in slots[1:]]
    by_rank = [None] + [rank_peer(rank) for rank in ranks[1:]]
    others, peers = pl.ds(0, nrow - 1), pl.ds(0, npair - 1)

    def copy_to(device, src, dst, ssem, rsem):
        return pltpu.make_async_remote_copy(
            src_ref=src, dst_ref=dst, send_sem=ssem, recv_sem=rsem,
            device_id=device, device_id_type=MESH,
        )

    plan_load = pltpu.make_async_copy(plan_hbm, plan_ref, in_sem.at[0])
    plan_load.start()
    barrier = pltpu.get_barrier_semaphore()
    for device in by_slot[1:] + by_rank[1:]:
        pl.semaphore_signal(barrier, inc=1, device_id=device, device_id_type=MESH)
    for j in range(nblocks):
        pltpu.make_async_copy(
            slab_ref.at[:, j * width : (j + 1) * width], xin.at[j], in_sem.at[1]
        ).start()
    plan_load.wait()

    def origin(edge, side):
        keep = plan_ref[1, 2 * edge + side]
        other = jnp.int32(0)
        sign = jnp.float32(0.0)
        for j in range(0, nblocks, 2):
            first, second = plan_ref[0, j], plan_ref[0, j + 1]
            other = jnp.where(first == keep, second, other)
            sign = jnp.where(first == keep, -1.0, sign)
            other = jnp.where(second == keep, first, other)
            sign = jnp.where(second == keep, 1.0, sign)
        return keep, other, sign

    pltpu.make_async_copy(xin, xin, in_sem.at[1]).wait()
    signs = []
    for side in range(2):
        for k in range(1, npair):
            keep, other, _ = origin(slots[k], side)
            send_f[side, k - 1, :, :width] = xin[keep]
            send_f[side, k - 1, :, width:] = xin[other]
        if side == 0:
            pl.semaphore_wait(barrier, nrow + npair - 2)
        for k in range(1, npair):
            copy_to(
                by_slot[k], send_f.at[side, k - 1], recv_f.at[side, p], f_send,
                f_recv.at[side],
            ).start()
    for side in range(2):
        keep, other, sign = origin(p, side)
        signs.append(sign)
        recv_f[side, p, :, :width] = xin[keep]
        recv_f[side, p, :, width:] = xin[other]

    def wait_recv(ref, sem):
        copy_to(by_rank[1], ref, ref, sem, sem).wait_recv()

    def wait_send(ref, sem):
        copy_to(by_rank[1], ref, ref, sem, sem).wait_send()

    def reduce_start(n, first, second):
        turned, right = first.T, split(second)
        band = width // CHUNKS
        for h in range(CHUNKS):
            left = split(turned[h * band : (h + 1) * band])
            part[n, h] = dot3(left, right).reshape(part.shape[2:])
            for k in range(1, nrow):
                copy_to(
                    by_rank[k], part.at[n, h, ranks[k]], gather_p.at[n, h, r], p_send,
                    p_recv.at[n, h],
                ).start()
        for h in range(CHUNKS):
            gather_p[n, h, r] = part[n, h, r]

    def squares_start(n, first, second):
        sums = jnp.concatenate(
            [
                jnp.sum(first * first, axis=0, keepdims=True),
                jnp.sum(second * second, axis=0, keepdims=True),
            ],
            axis=1,
        )
        for i in range(2 * half):
            dpart[n, i : i + 1, :] = sums[:, i * LANE : (i + 1) * LANE]
        for k in range(1, nrow):
            copy_to(
                by_rank[k], dpart.at[n], gather_d.at[n, r], d_send, d_recv.at[n]
            ).start()
        gather_d[n, r] = dpart[n]

    def reduce_middle(n):
        for h in range(CHUNKS):
            wait_recv(gather_p.at[n, h, others], p_recv.at[n, h])
            total = gather_p[n, h, 0]
            for j in range(1, nrow):
                total = total + gather_p[n, h, j]
            gram[n, h, r] = total
            for k in range(1, nrow):
                copy_to(
                    by_rank[k], gram.at[n, h, r], gram.at[n, h, r], g_send, g_recv.at[n]
                ).start()

    def denominator(n):
        wait_recv(gather_d.at[n, others], d_recv.at[n])
        sums = gather_d[n, 0]
        for j in range(1, nrow):
            sums = sums + gather_d[n, j]
        return column(sums, 0, width) + (line(sums, half, width) + 1e-6)

    def reduced(n):
        wait_recv(gram.at[n, :, others], g_recv.at[n])
        return gram[n].reshape(width, width)

    ident = (
        lax.broadcasted_iota(jnp.int32, (width, width), 0)
        == lax.broadcasted_iota(jnp.int32, (width, width), 1)
    ).astype(jnp.float32)

    def begin(couple, keep, other, sign):
        pieces = split(couple)
        scale = 1.0 + jnp.sum(couple * couple, keepdims=True)
        inv = 1.0 / scale
        inner = (ident + dot3(pieces, pieces, ROWS_BY_ROWS)) * inv
        mixed = keep + sign * dot3(split(other), pieces, ROWS_BY_ROWS)
        return inner, mixed * (0.5 * jnp.sqrt(inv))

    def factors_of(inner):
        product = None
        for step in range(NS_STEPS):
            factor = 1.5 * ident - 0.5 * inner
            fs = split(factor)
            product = 2.0 * factor if step == 0 else dot3(split(product), fs)
            if step + 1 < NS_STEPS:
                inner = dot3(split(dot3(split(inner), fs)), fs)
        return split(product)

    def rotate(items):
        inners, outs = [], []
        for item in items:
            inner, out = begin(*item)
            inners.append(inner)
            outs.append(2.0 * out)
        for step in range(NS_STEPS):
            factors = [split(1.5 * ident - 0.5 * inner) for inner in inners]
            if step + 1 == NS_STEPS:
                return [
                    functools.partial(dot3, split(out), fs)
                    for out, fs in zip(outs, factors)
                ]
            inners = [dot3(split(inner), fs) for inner, fs in zip(inners, factors)]
            outs = [dot3(split(out), fs) for out, fs in zip(outs, factors)]
            inners = [dot3(split(inner), fs) for inner, fs in zip(inners, factors)]

    for side in range(2):
        wait_recv(recv_f.at[side, peers], f_recv.at[side])
        both = recv_f[side].reshape(group, 2 * width)
        reduce_start(side, both[:, :width], both[:, width:])
        squares_start(side, both[:, :width], both[:, width:])
    denoms = []
    for side in range(2):
        reduce_middle(side)
        denoms.append(denominator(side))
    mixes, turns = [], []
    for side in range(2):
        couple = reduced(side) / denoms[side]
        both = recv_f[side].reshape(group, 2 * width)
        inner, mixed = begin(couple, both[:, :width], both[:, width:], signs[side])
        mixes.append(mixed)
        if side == 1:
            reduce_start(2, *mixes)
        turns.append(factors_of(inner))

    blocks = [dot3(split(mixed), turn) for mixed, turn in zip(mixes, turns)]
    squares_start(2, *blocks)
    reduce_middle(2)
    denom = denominator(2)
    middle = dot3(split(reduced(2)), turns[1])
    couple = dot3(turns[0], split(middle)) / denom
    lasts = rotate(
        [(couple, *blocks, -1.0), (couple.T, blocks[1], blocks[0], 1.0)]
    )
    for side in range(2):
        final = lasts[side]()
        send_b[side] = final.reshape(npair, rows, width)
        for k in range(1, npair):
            copy_to(
                by_slot[k], send_b.at[side, slots[k]], recv_b.at[2 * p + side], b_send,
                b_recv,
            ).start()
        sums = jnp.sum(final * final, axis=0, keepdims=True)
        for i in range(half):
            spart[side * half + i : side * half + i + 1, :] = sums[
                :, i * LANE : (i + 1) * LANE
            ]
    for k in range(1, nrow):
        copy_to(by_rank[k], spart, gather_s.at[r], s_send, s_recv).start()
    gather_s[r] = spart[...]
    mine = pl.ds(2 * p, 2)
    for side in range(2):
        recv_b[2 * p + side] = send_b[side, p]

    wait_recv(gather_s.at[others], s_recv)
    sums = gather_s[0]
    for j in range(1, nrow):
        sums = sums + gather_s[j]
    vals = jnp.sqrt(sums / total_rows)
    for side in range(2):
        sfin[side] = vals[side * half : (side + 1) * half]
    for k in range(1, npair):
        copy_to(by_slot[k], sfin, recv_s.at[mine], v_send, v_recv).start()
    recv_s[mine] = sfin[...]

    arrived = pl.ds(0, 2 * (npair - 1))
    wait_send(send_f.at[:, peers], f_send)
    wait_send(gather_d.at[:, others], d_send)
    wait_send(gather_p.at[:, :, others], p_send)
    wait_send(gram.at[:, :, others], g_send)
    wait_send(gather_s.at[others], s_send)
    wait_send(send_b.at[:, peers], b_send)
    wait_send(recv_s.at[arrived], v_send)
    wait_recv(recv_b.at[arrived], b_recv)
    wait_recv(recv_s.at[arrived], v_recv)
    for j in range(nblocks):
        slot = locate(plan_ref, j, nblocks)
        out_ref[:, j * width : (j + 1) * width] = recv_b[slot]
        vals_ref[j * half : (j + 1) * half, :] = recv_s[slot]


def solution(mesh):
    nrow, npair = mesh.shape["row"], mesh.shape["pair"]
    vmem, smem = pltpu.VMEM, pltpu.SMEM
    anywhere = pl.BlockSpec(memory_space=pl.ANY)

    def on_device(slab, plan):
        rows, ncols = slab.shape
        nblocks = 2 * npair
        width = ncols // nblocks
        part_rows = width // (nrow * CHUNKS)
        half = width // LANE
        f32 = jnp.float32
        dma = pltpu.SemaphoreType.DMA
        out, vals = pl.pallas_call(
            functools.partial(kernel, rows * nrow * npair),
            out_shape=(
                pltpu.VMEM((rows, ncols), f32),
                pltpu.VMEM((nblocks * half, LANE), f32),
            ),
            in_specs=[anywhere, anywhere],
            out_specs=(pl.BlockSpec(memory_space=vmem), pl.BlockSpec(memory_space=vmem)),
            scratch_shapes=[
                vmem((nblocks, rows, width), f32),
                vmem((nblocks, half, LANE), f32),
                smem(plan.shape, jnp.int32),
                vmem((nblocks, rows, width), f32),
                vmem((2, npair - 1, rows, 2 * width), f32),
                vmem((2, npair, rows, 2 * width), f32),
                vmem((3, CHUNKS, nrow, part_rows, width), f32),
                vmem((3, CHUNKS, nrow, part_rows, width), f32),
                vmem((3, 2 * half, LANE), f32),
                vmem((3, nrow, 2 * half, LANE), f32),
                vmem((3, CHUNKS, nrow, part_rows, width), f32),
                vmem((2, npair, rows, width), f32),
                vmem((2 * half, LANE), f32),
                vmem((nrow, 2 * half, LANE), f32),
                vmem((2, half, LANE), f32),
                dma((2,)),
                dma,
                dma((2,)),
                dma,
                dma((3, CHUNKS)),
                dma,
                dma((3,)),
                dma,
                dma((3,)),
                dma,
                dma,
                dma,
                dma,
                dma,
                dma,
            ],
            compiler_params=pltpu.CompilerParams(
                collective_id=0, has_side_effects=True, vmem_limit_bytes=66000000
            ),
        )(plan, slab)
        return out, vals.reshape(ncols)

    return jax.shard_map(
        on_device,
        mesh=mesh,
        in_specs=(P(("row", "pair"), None), P()),
        out_specs=(P(("row", "pair"), None), P()),
        check_vma=False,
    )
```

```python
import functools

import jax
import jax.numpy as jnp
from jax import lax
from jax.experimental import pallas as pl
from jax.experimental.pallas import tpu as pltpu
from jax.sharding import PartitionSpec as P

NS_STEPS = 4
CHUNKS = 2
MESH = pl.DeviceIdType.MESH
LANE = 128
ROWS_BY_ROWS = (((1,), (1,)), ((), ()))
PLAIN = (((1,), (0,)), ((), ()))


def split(x):
    high = x.astype(jnp.bfloat16)
    low = (x - high.astype(jnp.float32)).astype(jnp.bfloat16)
    return high, low


def dot3(a, b, dims=PLAIN):
    (ah, al), (bh, bl) = a, b
    mul = functools.partial(
        lax.dot_general, dimension_numbers=dims, preferred_element_type=jnp.float32
    )
    return mul(ah, bh) + (mul(ah, bl) + mul(al, bh))


def column(tile, first, width):
    turned = tile.T
    return jnp.concatenate(
        [turned[:, first + i : first + i + 1] for i in range(width // LANE)], axis=0
    )


def line(tile, first, width):
    return jnp.concatenate(
        [tile[first + i : first + i + 1, :] for i in range(width // LANE)], axis=1
    )


def ring_places(r, p, nrow, npair):
    def slot_peer(slot):
        return {"row": r, "pair": slot}

    def rank_peer(rank):
        return {"row": rank, "pair": p}

    return p, r, slot_peer, rank_peer


def torus_places(r, p):
    core, y_lo, z = lax.rem(r, 2), lax.rem(lax.div(r, 2), 2), lax.div(r, 4)
    y_hi, x = lax.div(p, 4), lax.rem(p, 4)
    y = 2 * y_hi + y_lo

    def device(x, y, z, core):
        return {
            "row": (z * 2 + lax.rem(y, 2)) * 2 + core,
            "pair": lax.div(y, 2) * 4 + x,
        }

    inner = y_lo != y_hi

    def slot_peer(slot):
        h, xx = lax.div(slot, 4), lax.rem(slot, 4)
        return device(xx, jnp.where(inner, 1 + h, 3 * h), z, core)

    def rank_peer(m):
        return device(x, 2 * y_hi + lax.rem(lax.div(m, 2), 2), lax.div(m, 4), lax.rem(m, 2))

    return p, r, slot_peer, rank_peer


def locate(plan_ref, block, nblocks):
    slot = jnp.int32(0)
    for j in range(nblocks):
        slot = jnp.where(plan_ref[1, j] == block, j, slot)
    return slot


def kernel(
    total_rows,
    plan_hbm,
    slab_ref,
    out_ref,
    vals_ref,
    recv_b,
    recv_s,
    plan_ref,
    xin,
    send_f,
    recv_f,
    part,
    gather_p,
    dpart,
    gather_d,
    gram,
    send_b,
    spart,
    gather_s,
    sfin,
    in_sem,
    f_send,
    f_recv,
    p_send,
    p_recv,
    d_send,
    d_recv,
    g_send,
    g_recv,
    b_send,
    b_recv,
    s_send,
    s_recv,
    v_send,
    v_recv,
):
    nrow, npair = lax.axis_size("row"), lax.axis_size("pair")
    row, pair = lax.axis_index("row"), lax.axis_index("pair")
    nblocks = 2 * npair
    rows, width = xin.shape[1:]
    half = width // LANE
    group = npair * rows
    if (nrow, npair) == (16, 8):
        p, r, slot_peer, rank_peer = torus_places(row, pair)
    else:
        p, r, slot_peer, rank_peer = ring_places(row, pair, nrow, npair)
    slots = [lax.rem(p + k, npair) for k in range(npair)]
    ranks = [lax.rem(r + k, nrow) for k in range(nrow)]
    if (nrow, npair) == (16, 8):
        far_first = (2, 1, 3, 0)
        slots = [
            lax.rem(lax.div(p, 4) + dy, 2) * 4 + lax.rem(p + dx, 4)
            for dx in far_first
            for dy in (1, 0)
            if dx or dy
        ]
        slots = [p] + slots
        ranks = [
            (lax.rem(lax.div(r, 4) + dz, 4) * 2 + lax.rem(lax.div(r, 2) + dy, 2)) * 2
            + lax.rem(r + dc, 2)
            for dz in far_first
            for dy in (1, 0)
            for dc in (1, 0)
            if dz or dy or dc
        ]
        ranks = [r] + ranks
    by_slot = [None] + [slot_peer(slot) for slot in slots[1:]]
    by_rank = [None] + [rank_peer(rank) for rank in ranks[1:]]
    others, peers = pl.ds(0, nrow - 1), pl.ds(0, npair - 1)

    def copy_to(device, src, dst, ssem, rsem):
        return pltpu.make_async_remote_copy(
            src_ref=src, dst_ref=dst, send_sem=ssem, recv_sem=rsem,
            device_id=device, device_id_type=MESH,
        )

    plan_load = pltpu.make_async_copy(plan_hbm, plan_ref, in_sem.at[0])
    plan_load.start()
    barrier = pltpu.get_barrier_semaphore()
    for device in by_slot[1:] + by_rank[1:]:
        pl.semaphore_signal(barrier, inc=1, device_id=device, device_id_type=MESH)
    for j in range(nblocks):
        pltpu.make_async_copy(
            slab_ref.at[:, j * width : (j + 1) * width], xin.at[j], in_sem.at[1]
        ).start()
    plan_load.wait()

    def origin(edge, side):
        keep = plan_ref[1, 2 * edge + side]
        other = jnp.int32(0)
        sign = jnp.float32(0.0)
        for j in range(0, nblocks, 2):
            first, second = plan_ref[0, j], plan_ref[0, j + 1]
            other = jnp.where(first == keep, second, other)
            sign = jnp.where(first == keep, -1.0, sign)
            other = jnp.where(second == keep, first, other)
            sign = jnp.where(second == keep, 1.0, sign)
        return keep, other, sign

    pltpu.make_async_copy(xin, xin, in_sem.at[1]).wait()
    signs = []
    for side in range(2):
        for k in range(1, npair):
            keep, other, _ = origin(slots[k], side)
            send_f[side, k - 1, :, :width] = xin[keep]
            send_f[side, k - 1, :, width:] = xin[other]
        if side == 0:
            pl.semaphore_wait(barrier, nrow + npair - 2)
        for k in range(1, npair):
            copy_to(
                by_slot[k], send_f.at[side, k - 1], recv_f.at[side, p], f_send,
                f_recv.at[side],
            ).start()
    for side in range(2):
        keep, other, sign = origin(p, side)
        signs.append(sign)
        recv_f[side, p, :, :width] = xin[keep]
        recv_f[side, p, :, width:] = xin[other]

    def wait_recv(ref, sem):
        copy_to(by_rank[1], ref, ref, sem, sem).wait_recv()

    def wait_send(ref, sem):
        copy_to(by_rank[1], ref, ref, sem, sem).wait_send()

    def reduce_start(n, first, second):
        turned, right = first.T, split(second)
        band = width // CHUNKS
        for h in range(CHUNKS):
            left = split(turned[h * band : (h + 1) * band])
            part[n, h] = dot3(left, right).reshape(part.shape[2:])
            for k in range(1, nrow):
                copy_to(
                    by_rank[k], part.at[n, h, ranks[k]], gather_p.at[n, h, r], p_send,
                    p_recv.at[n, h],
                ).start()
        for h in range(CHUNKS):
            gather_p[n, h, r] = part[n, h, r]

    def squares_start(n, first, second):
        sums = jnp.concatenate(
            [
                jnp.sum(first * first, axis=0, keepdims=True),
                jnp.sum(second * second, axis=0, keepdims=True),
            ],
            axis=1,
        )
        for i in range(2 * half):
            dpart[n, i : i + 1, :] = sums[:, i * LANE : (i + 1) * LANE]
        for k in range(1, nrow):
            copy_to(
                by_rank[k], dpart.at[n], gather_d.at[n, r], d_send, d_recv.at[n]
            ).start()
        gather_d[n, r] = dpart[n]

    def reduce_middle(n):
        for h in range(CHUNKS):
            wait_recv(gather_p.at[n, h, others], p_recv.at[n, h])
            total = gather_p[n, h, 0]
            for j in range(1, nrow):
                total = total + gather_p[n, h, j]
            gram[n, h, r] = total
            for k in range(1, nrow):
                copy_to(
                    by_rank[k], gram.at[n, h, r], gram.at[n, h, r], g_send, g_recv.at[n]
                ).start()

    def denominator(n):
        wait_recv(gather_d.at[n, others], d_recv.at[n])
        sums = gather_d[n, 0]
        for j in range(1, nrow):
            sums = sums + gather_d[n, j]
        return column(sums, 0, width) + (line(sums, half, width) + 1e-6)

    def reduced(n):
        wait_recv(gram.at[n, :, others], g_recv.at[n])
        return gram[n].reshape(width, width)

    ident = (
        lax.broadcasted_iota(jnp.int32, (width, width), 0)
        == lax.broadcasted_iota(jnp.int32, (width, width), 1)
    ).astype(jnp.float32)

    def begin(couple, keep, other, sign):
        pieces = split(couple)
        scale = 1.0 + jnp.sum(couple * couple, keepdims=True)
        inv = 1.0 / scale
        inner = (ident + dot3(pieces, pieces, ROWS_BY_ROWS)) * inv
        mixed = keep + sign * dot3(split(other), pieces, ROWS_BY_ROWS)
        return inner, mixed * (0.5 * jnp.sqrt(inv))

    def factors_of(inner):
        product = None
        for step in range(NS_STEPS):
            factor = 1.5 * ident - 0.5 * inner
            fs = split(factor)
            product = 2.0 * factor if step == 0 else dot3(split(product), fs)
            if step + 1 < NS_STEPS:
                inner = dot3(split(dot3(split(inner), fs)), fs)
        return split(product)

    def rotate(items):
        inners, outs = [], []
        for item in items:
            inner, out = begin(*item)
            inners.append(inner)
            outs.append(2.0 * out)
        for step in range(NS_STEPS):
            factors = [split(1.5 * ident - 0.5 * inner) for inner in inners]
            if step + 1 == NS_STEPS:
                return [
                    functools.partial(dot3, split(out), fs)
                    for out, fs in zip(outs, factors)
                ]
            inners = [dot3(split(inner), fs) for inner, fs in zip(inners, factors)]
            outs = [dot3(split(out), fs) for out, fs in zip(outs, factors)]
            inners = [dot3(split(inner), fs) for inner, fs in zip(inners, factors)]

    wait_recv(recv_f.at[0, peers], f_recv.at[0])
    both = recv_f[0].reshape(group, 2 * width)
    reduce_start(0, both[:, :width], both[:, width:])
    both = recv_f[0].reshape(group, 2 * width)
    squares_start(0, both[:, :width], both[:, width:])
    wait_recv(recv_f.at[1, peers], f_recv.at[1])
    both = recv_f[1].reshape(group, 2 * width)
    reduce_start(1, both[:, :width], both[:, width:])
    both = recv_f[1].reshape(group, 2 * width)
    squares_start(1, both[:, :width], both[:, width:])
    reduce_middle(0)
    reduce_middle(1)
    denoms = [denominator(side) for side in range(2)]

    mixes, turns = [], []
    for side in range(2):
        couple = reduced(side) / denoms[side]
        both = recv_f[side].reshape(group, 2 * width)
        inner, mixed = begin(couple, both[:, :width], both[:, width:], signs[side])
        mixes.append(mixed)
        if side == 1:
            reduce_start(2, *mixes)
        turns.append(factors_of(inner))

    blocks = [dot3(split(mixed), turn) for mixed, turn in zip(mixes, turns)]
    squares_start(2, *blocks)
    reduce_middle(2)
    denom = denominator(2)
    middle = dot3(split(reduced(2)), turns[1])
    couple = dot3(turns[0], split(middle)) / denom
    lasts = rotate(
        [(couple, *blocks, -1.0), (couple.T, blocks[1], blocks[0], 1.0)]
    )
    for side in range(2):
        final = lasts[side]()
        send_b[side] = final.reshape(npair, rows, width)
        for k in range(1, npair):
            copy_to(
                by_slot[k], send_b.at[side, slots[k]], recv_b.at[2 * p + side], b_send,
                b_recv,
            ).start()
        sums = jnp.sum(final * final, axis=0, keepdims=True)
        for i in range(half):
            spart[side * half + i : side * half + i + 1, :] = sums[
                :, i * LANE : (i + 1) * LANE
            ]
    for k in range(1, nrow):
        copy_to(by_rank[k], spart, gather_s.at[r], s_send, s_recv).start()
    gather_s[r] = spart[...]
    mine = pl.ds(2 * p, 2)
    for side in range(2):
        recv_b[2 * p + side] = send_b[side, p]

    wait_recv(gather_s.at[others], s_recv)
    sums = gather_s[0]
    for j in range(1, nrow):
        sums = sums + gather_s[j]
    vals = jnp.sqrt(sums / total_rows)
    for side in range(2):
        sfin[side] = vals[side * half : (side + 1) * half]
    for k in range(1, npair):
        copy_to(by_slot[k], sfin, recv_s.at[mine], v_send, v_recv).start()
    recv_s[mine] = sfin[...]

    arrived = pl.ds(0, 2 * (npair - 1))
    wait_send(send_f.at[:, peers], f_send)
    wait_send(gather_d.at[:, others], d_send)
    wait_send(gather_p.at[:, :, others], p_send)
    wait_send(gram.at[:, :, others], g_send)
    wait_send(gather_s.at[others], s_send)
    wait_send(send_b.at[:, peers], b_send)
    wait_send(recv_s.at[arrived], v_send)
    wait_recv(recv_b.at[arrived], b_recv)
    wait_recv(recv_s.at[arrived], v_recv)
    for j in range(nblocks):
        slot = locate(plan_ref, j, nblocks)
        out_ref[:, j * width : (j + 1) * width] = recv_b[slot]
        vals_ref[j * half : (j + 1) * half, :] = recv_s[slot]


def solution(mesh):
    nrow, npair = mesh.shape["row"], mesh.shape["pair"]
    vmem, smem = pltpu.VMEM, pltpu.SMEM
    anywhere = pl.BlockSpec(memory_space=pl.ANY)

    def on_device(slab, plan):
        rows, ncols = slab.shape
        nblocks = 2 * npair
        width = ncols // nblocks
        part_rows = width // (nrow * CHUNKS)
        half = width // LANE
        f32 = jnp.float32
        dma = pltpu.SemaphoreType.DMA
        out, vals = pl.pallas_call(
            functools.partial(kernel, rows * nrow * npair),
            out_shape=(
                pltpu.VMEM((rows, ncols), f32),
                pltpu.VMEM((nblocks * half, LANE), f32),
            ),
            in_specs=[anywhere, anywhere],
            out_specs=(pl.BlockSpec(memory_space=vmem), pl.BlockSpec(memory_space=vmem)),
            scratch_shapes=[
                vmem((nblocks, rows, width), f32),
                vmem((nblocks, half, LANE), f32),
                smem(plan.shape, jnp.int32),
                vmem((nblocks, rows, width), f32),
                vmem((2, npair - 1, rows, 2 * width), f32),
                vmem((2, npair, rows, 2 * width), f32),
                vmem((3, CHUNKS, nrow, part_rows, width), f32),
                vmem((3, CHUNKS, nrow, part_rows, width), f32),
                vmem((3, 2 * half, LANE), f32),
                vmem((3, nrow, 2 * half, LANE), f32),
                vmem((3, CHUNKS, nrow, part_rows, width), f32),
                vmem((2, npair, rows, width), f32),
                vmem((2 * half, LANE), f32),
                vmem((nrow, 2 * half, LANE), f32),
                vmem((2, half, LANE), f32),
                dma((2,)),
                dma,
                dma((2,)),
                dma,
                dma((3, CHUNKS)),
                dma,
                dma((3,)),
                dma,
                dma((3,)),
                dma,
                dma,
                dma,
                dma,
                dma,
                dma,
            ],
            compiler_params=pltpu.CompilerParams(
                collective_id=0, has_side_effects=True, vmem_limit_bytes=66000000
            ),
        )(plan, slab)
        return out, vals.reshape(ncols)

    return jax.shard_map(
        on_device,
        mesh=mesh,
        in_specs=(P(("row", "pair"), None), P()),
        out_specs=(P(("row", "pair"), None), P()),
        check_vma=False,
    )
```

```python
import functools

import jax
import jax.numpy as jnp
from jax import lax
from jax.experimental import pallas as pl
from jax.experimental.pallas import tpu as pltpu
from jax.sharding import PartitionSpec as P

NS_STEPS = 4
CHUNKS = 2
MESH = pl.DeviceIdType.MESH
LANE = 128
ROWS_BY_ROWS = (((1,), (1,)), ((), ()))
PLAIN = (((1,), (0,)), ((), ()))


def split(x):
    high = x.astype(jnp.bfloat16)
    low = (x - high.astype(jnp.float32)).astype(jnp.bfloat16)
    return high, low


def dot3(a, b, dims=PLAIN):
    (ah, al), (bh, bl) = a, b
    mul = functools.partial(
        lax.dot_general, dimension_numbers=dims, preferred_element_type=jnp.float32
    )
    return mul(ah, bh) + (mul(ah, bl) + mul(al, bh))


def column(tile, first, width):
    turned = tile.T
    return jnp.concatenate(
        [turned[:, first + i : first + i + 1] for i in range(width // LANE)], axis=0
    )


def line(tile, first, width):
    return jnp.concatenate(
        [tile[first + i : first + i + 1, :] for i in range(width // LANE)], axis=1
    )


def ring_places(r, p, nrow, npair):
    def slot_peer(slot):
        return {"row": r, "pair": slot}

    def rank_peer(rank):
        return {"row": rank, "pair": p}

    return p, r, slot_peer, rank_peer


def torus_places(r, p):
    core, y_lo, z = lax.rem(r, 2), lax.rem(lax.div(r, 2), 2), lax.div(r, 4)
    y_hi, x = lax.div(p, 4), lax.rem(p, 4)
    y = 2 * y_hi + y_lo

    def device(x, y, z, core):
        return {
            "row": (z * 2 + lax.rem(y, 2)) * 2 + core,
            "pair": lax.div(y, 2) * 4 + x,
        }

    inner = y_lo != y_hi

    def slot_peer(slot):
        h, xx = lax.div(slot, 4), lax.rem(slot, 4)
        return device(xx, jnp.where(inner, 1 + h, 3 * h), z, core)

    def rank_peer(m):
        return device(x, 2 * y_hi + lax.rem(lax.div(m, 2), 2), lax.div(m, 4), lax.rem(m, 2))

    return p, r, slot_peer, rank_peer


def locate(plan_ref, block, nblocks):
    slot = jnp.int32(0)
    for j in range(nblocks):
        slot = jnp.where(plan_ref[1, j] == block, j, slot)
    return slot


def kernel(
    total_rows,
    plan_hbm,
    slab_ref,
    out_ref,
    vals_ref,
    recv_b,
    recv_s,
    plan_ref,
    xin,
    send_f,
    recv_f,
    part,
    gather_p,
    dpart,
    gather_d,
    gram,
    send_b,
    spart,
    gather_s,
    sfin,
    in_sem,
    f_send,
    f_recv,
    p_send,
    p_recv,
    d_send,
    d_recv,
    g_send,
    g_recv,
    b_send,
    b_recv,
    s_send,
    s_recv,
    v_send,
    v_recv,
):
    nrow, npair = lax.axis_size("row"), lax.axis_size("pair")
    row, pair = lax.axis_index("row"), lax.axis_index("pair")
    nblocks = 2 * npair
    rows, width = xin.shape[1:]
    half = width // LANE
    group = npair * rows
    if (nrow, npair) == (16, 8):
        p, r, slot_peer, rank_peer = torus_places(row, pair)
    else:
        p, r, slot_peer, rank_peer = ring_places(row, pair, nrow, npair)
    slots = [lax.rem(p + k, npair) for k in range(npair)]
    ranks = [lax.rem(r + k, nrow) for k in range(nrow)]
    if (nrow, npair) == (16, 8):
        far_first = ((2, 1), (2, 0), (1, 1), (3, 1), (1, 0), (3, 0), (0, 1), (0, 0))
        slots = [
            lax.rem(lax.div(p, 4) + dy, 2) * 4 + lax.rem(p + dx, 4)
            for dx, dy in far_first
            if dx or dy
        ]
        slots = [p] + slots
        ranks = [
            (lax.rem(lax.div(r, 4) + dz, 4) * 2 + lax.rem(lax.div(r, 2) + dy, 2)) * 2
            + lax.rem(r + dc, 2)
            for dz, dy in far_first
            for dc in (1, 0)
            if dz or dy or dc
        ]
        ranks = [r] + ranks
    by_slot = [None] + [slot_peer(slot) for slot in slots[1:]]
    by_rank = [None] + [rank_peer(rank) for rank in ranks[1:]]
    others, peers = pl.ds(0, nrow - 1), pl.ds(0, npair - 1)

    def copy_to(device, src, dst, ssem, rsem):
        return pltpu.make_async_remote_copy(
            src_ref=src, dst_ref=dst, send_sem=ssem, recv_sem=rsem,
            device_id=device, device_id_type=MESH,
        )

    plan_load = pltpu.make_async_copy(plan_hbm, plan_ref, in_sem.at[0])
    plan_load.start()
    barrier = pltpu.get_barrier_semaphore()
    for device in by_slot[1:] + by_rank[1:]:
        pl.semaphore_signal(barrier, inc=1, device_id=device, device_id_type=MESH)
    for j in range(nblocks):
        pltpu.make_async_copy(
            slab_ref.at[:, j * width : (j + 1) * width], xin.at[j], in_sem.at[1]
        ).start()
    plan_load.wait()

    def origin(edge, side):
        keep = plan_ref[1, 2 * edge + side]
        other = jnp.int32(0)
        sign = jnp.float32(0.0)
        for j in range(0, nblocks, 2):
            first, second = plan_ref[0, j], plan_ref[0, j + 1]
            other = jnp.where(first == keep, second, other)
            sign = jnp.where(first == keep, -1.0, sign)
            other = jnp.where(second == keep, first, other)
            sign = jnp.where(second == keep, 1.0, sign)
        return keep, other, sign

    pltpu.make_async_copy(xin, xin, in_sem.at[1]).wait()
    signs = []
    for side in range(2):
        for k in range(1, npair):
            keep, other, _ = origin(slots[k], side)
            send_f[side, k - 1, :, :width] = xin[keep]
            send_f[side, k - 1, :, width:] = xin[other]
        if side == 0:
            pl.semaphore_wait(barrier, nrow + npair - 2)
        for k in range(1, npair):
            copy_to(
                by_slot[k], send_f.at[side, k - 1], recv_f.at[side, p], f_send,
                f_recv.at[side],
            ).start()
    for side in range(2):
        keep, other, sign = origin(p, side)
        signs.append(sign)
        recv_f[side, p, :, :width] = xin[keep]
        recv_f[side, p, :, width:] = xin[other]

    def wait_recv(ref, sem):
        copy_to(by_rank[1], ref, ref, sem, sem).wait_recv()

    def wait_send(ref, sem):
        copy_to(by_rank[1], ref, ref, sem, sem).wait_send()

    def reduce_start(n, first, second):
        turned, right = first.T, split(second)
        band = width // CHUNKS
        for h in range(CHUNKS):
            left = split(turned[h * band : (h + 1) * band])
            part[n, h] = dot3(left, right).reshape(part.shape[2:])
            for k in range(1, nrow):
                copy_to(
                    by_rank[k], part.at[n, h, ranks[k]], gather_p.at[n, h, r], p_send,
                    p_recv.at[n, h],
                ).start()
        for h in range(CHUNKS):
            gather_p[n, h, r] = part[n, h, r]

    def squares_start(n, first, second):
        sums = jnp.concatenate(
            [
                jnp.sum(first * first, axis=0, keepdims=True),
                jnp.sum(second * second, axis=0, keepdims=True),
            ],
            axis=1,
        )
        for i in range(2 * half):
            dpart[n, i : i + 1, :] = sums[:, i * LANE : (i + 1) * LANE]
        for k in range(1, nrow):
            copy_to(
                by_rank[k], dpart.at[n], gather_d.at[n, r], d_send, d_recv.at[n]
            ).start()
        gather_d[n, r] = dpart[n]

    def reduce_middle(n):
        for h in range(CHUNKS):
            wait_recv(gather_p.at[n, h, others], p_recv.at[n, h])
            total = gather_p[n, h, 0]
            for j in range(1, nrow):
                total = total + gather_p[n, h, j]
            gram[n, h, r] = total
            for k in range(1, nrow):
                copy_to(
                    by_rank[k], gram.at[n, h, r], gram.at[n, h, r], g_send, g_recv.at[n]
                ).start()

    def denominator(n):
        wait_recv(gather_d.at[n, others], d_recv.at[n])
        sums = gather_d[n, 0]
        for j in range(1, nrow):
            sums = sums + gather_d[n, j]
        return column(sums, 0, width) + (line(sums, half, width) + 1e-6)

    def reduced(n):
        wait_recv(gram.at[n, :, others], g_recv.at[n])
        return gram[n].reshape(width, width)

    ident = (
        lax.broadcasted_iota(jnp.int32, (width, width), 0)
        == lax.broadcasted_iota(jnp.int32, (width, width), 1)
    ).astype(jnp.float32)

    def begin(couple, keep, other, sign):
        pieces = split(couple)
        scale = 1.0 + jnp.sum(couple * couple, keepdims=True)
        inv = 1.0 / scale
        inner = (ident + dot3(pieces, pieces, ROWS_BY_ROWS)) * inv
        mixed = keep + sign * dot3(split(other), pieces, ROWS_BY_ROWS)
        return inner, mixed * (0.5 * jnp.sqrt(inv))

    def factors_of(inner):
        product = None
        for step in range(NS_STEPS):
            factor = 1.5 * ident - 0.5 * inner
            fs = split(factor)
            product = 2.0 * factor if step == 0 else dot3(split(product), fs)
            if step + 1 < NS_STEPS:
                inner = dot3(split(dot3(split(inner), fs)), fs)
        return split(product)

    def rotate(items):
        inners, outs = [], []
        for item in items:
            inner, out = begin(*item)
            inners.append(inner)
            outs.append(2.0 * out)
        for step in range(NS_STEPS):
            factors = [split(1.5 * ident - 0.5 * inner) for inner in inners]
            if step + 1 == NS_STEPS:
                return [
                    functools.partial(dot3, split(out), fs)
                    for out, fs in zip(outs, factors)
                ]
            inners = [dot3(split(inner), fs) for inner, fs in zip(inners, factors)]
            outs = [dot3(split(out), fs) for out, fs in zip(outs, factors)]
            inners = [dot3(split(inner), fs) for inner, fs in zip(inners, factors)]

    wait_recv(recv_f.at[0, peers], f_recv.at[0])
    both = recv_f[0].reshape(group, 2 * width)
    reduce_start(0, both[:, :width], both[:, width:])
    both = recv_f[0].reshape(group, 2 * width)
    squares_start(0, both[:, :width], both[:, width:])
    wait_recv(recv_f.at[1, peers], f_recv.at[1])
    both = recv_f[1].reshape(group, 2 * width)
    reduce_start(1, both[:, :width], both[:, width:])
    both = recv_f[1].reshape(group, 2 * width)
    squares_start(1, both[:, :width], both[:, width:])
    reduce_middle(0)
    reduce_middle(1)
    denoms = [denominator(side) for side in range(2)]

    mixes, turns = [], []
    for side in range(2):
        couple = reduced(side) / denoms[side]
        both = recv_f[side].reshape(group, 2 * width)
        inner, mixed = begin(couple, both[:, :width], both[:, width:], signs[side])
        mixes.append(mixed)
        if side == 1:
            reduce_start(2, *mixes)
        turns.append(factors_of(inner))

    blocks = [dot3(split(mixed), turn) for mixed, turn in zip(mixes, turns)]
    squares_start(2, *blocks)
    reduce_middle(2)
    denom = denominator(2)
    middle = dot3(split(reduced(2)), turns[1])
    couple = dot3(turns[0], split(middle)) / denom
    lasts = rotate(
        [(couple, *blocks, -1.0), (couple.T, blocks[1], blocks[0], 1.0)]
    )
    for side in range(2):
        final = lasts[side]()
        send_b[side] = final.reshape(npair, rows, width)
        for k in range(1, npair):
            copy_to(
                by_slot[k], send_b.at[side, slots[k]], recv_b.at[2 * p + side], b_send,
                b_recv,
            ).start()
        sums = jnp.sum(final * final, axis=0, keepdims=True)
        for i in range(half):
            spart[side * half + i : side * half + i + 1, :] = sums[
                :, i * LANE : (i + 1) * LANE
            ]
    for k in range(1, nrow):
        copy_to(by_rank[k], spart, gather_s.at[r], s_send, s_recv).start()
    gather_s[r] = spart[...]
    mine = pl.ds(2 * p, 2)
    for side in range(2):
        recv_b[2 * p + side] = send_b[side, p]

    wait_recv(gather_s.at[others], s_recv)
    sums = gather_s[0]
    for j in range(1, nrow):
        sums = sums + gather_s[j]
    vals = jnp.sqrt(sums / total_rows)
    for side in range(2):
        sfin[side] = vals[side * half : (side + 1) * half]
    for k in range(1, npair):
        copy_to(by_slot[k], sfin, recv_s.at[mine], v_send, v_recv).start()
    recv_s[mine] = sfin[...]

    arrived = pl.ds(0, 2 * (npair - 1))
    wait_send(send_f.at[:, peers], f_send)
    wait_send(gather_d.at[:, others], d_send)
    wait_send(gather_p.at[:, :, others], p_send)
    wait_send(gram.at[:, :, others], g_send)
    wait_send(gather_s.at[others], s_send)
    wait_send(send_b.at[:, peers], b_send)
    wait_send(recv_s.at[arrived], v_send)
    wait_recv(recv_b.at[arrived], b_recv)
    wait_recv(recv_s.at[arrived], v_recv)
    for j in range(nblocks):
        slot = locate(plan_ref, j, nblocks)
        out_ref[:, j * width : (j + 1) * width] = recv_b[slot]
        vals_ref[j * half : (j + 1) * half, :] = recv_s[slot]


def solution(mesh):
    nrow, npair = mesh.shape["row"], mesh.shape["pair"]
    vmem, smem = pltpu.VMEM, pltpu.SMEM
    anywhere = pl.BlockSpec(memory_space=pl.ANY)

    def on_device(slab, plan):
        rows, ncols = slab.shape
        nblocks = 2 * npair
        width = ncols // nblocks
        part_rows = width // (nrow * CHUNKS)
        half = width // LANE
        f32 = jnp.float32
        dma = pltpu.SemaphoreType.DMA
        out, vals = pl.pallas_call(
            functools.partial(kernel, rows * nrow * npair),
            out_shape=(
                pltpu.VMEM((rows, ncols), f32),
                pltpu.VMEM((nblocks * half, LANE), f32),
            ),
            in_specs=[anywhere, anywhere],
            out_specs=(pl.BlockSpec(memory_space=vmem), pl.BlockSpec(memory_space=vmem)),
            scratch_shapes=[
                vmem((nblocks, rows, width), f32),
                vmem((nblocks, half, LANE), f32),
                smem(plan.shape, jnp.int32),
                vmem((nblocks, rows, width), f32),
                vmem((2, npair - 1, rows, 2 * width), f32),
                vmem((2, npair, rows, 2 * width), f32),
                vmem((3, CHUNKS, nrow, part_rows, width), f32),
                vmem((3, CHUNKS, nrow, part_rows, width), f32),
                vmem((3, 2 * half, LANE), f32),
                vmem((3, nrow, 2 * half, LANE), f32),
                vmem((3, CHUNKS, nrow, part_rows, width), f32),
                vmem((2, npair, rows, width), f32),
                vmem((2 * half, LANE), f32),
                vmem((nrow, 2 * half, LANE), f32),
                vmem((2, half, LANE), f32),
                dma((2,)),
                dma,
                dma((2,)),
                dma,
                dma((3, CHUNKS)),
                dma,
                dma((3,)),
                dma,
                dma((3,)),
                dma,
                dma,
                dma,
                dma,
                dma,
                dma,
            ],
            compiler_params=pltpu.CompilerParams(
                collective_id=0, has_side_effects=True, vmem_limit_bytes=66000000
            ),
        )(plan, slab)
        return out, vals.reshape(ncols)

    return jax.shard_map(
        on_device,
        mesh=mesh,
        in_specs=(P(("row", "pair"), None), P()),
        out_specs=(P(("row", "pair"), None), P()),
        check_vma=False,
    )
```

```python
import functools

import jax
import jax.numpy as jnp
from jax import lax
from jax.experimental import pallas as pl
from jax.experimental.pallas import tpu as pltpu
from jax.sharding import PartitionSpec as P

NS_STEPS = 4
BANDS, HALVES = 2, 2
CHUNKS = BANDS * HALVES
MESH = pl.DeviceIdType.MESH
LANE = 128
ROWS_BY_ROWS = (((1,), (1,)), ((), ()))
PLAIN = (((1,), (0,)), ((), ()))


def split(x):
    high = x.astype(jnp.bfloat16)
    low = (x - high.astype(jnp.float32)).astype(jnp.bfloat16)
    return high, low


def dot3(a, b, dims=PLAIN):
    (ah, al), (bh, bl) = a, b
    mul = functools.partial(
        lax.dot_general, dimension_numbers=dims, preferred_element_type=jnp.float32
    )
    return mul(ah, bh) + (mul(ah, bl) + mul(al, bh))


def column(tile, first, width):
    turned = tile.T
    return jnp.concatenate(
        [turned[:, first + i : first + i + 1] for i in range(width // LANE)], axis=0
    )


def line(tile, first, width):
    return jnp.concatenate(
        [tile[first + i : first + i + 1, :] for i in range(width // LANE)], axis=1
    )


def ring_places(r, p, nrow, npair):
    def slot_peer(slot):
        return {"row": r, "pair": slot}

    def rank_peer(rank):
        return {"row": rank, "pair": p}

    return p, r, slot_peer, rank_peer


def torus_places(r, p):
    core, y_lo, z = lax.rem(r, 2), lax.rem(lax.div(r, 2), 2), lax.div(r, 4)
    y_hi, x = lax.div(p, 4), lax.rem(p, 4)
    y = 2 * y_hi + y_lo

    def device(x, y, z, core):
        return {
            "row": (z * 2 + lax.rem(y, 2)) * 2 + core,
            "pair": lax.div(y, 2) * 4 + x,
        }

    inner = y_lo != y_hi

    def slot_peer(slot):
        h, xx = lax.div(slot, 4), lax.rem(slot, 4)
        return device(xx, jnp.where(inner, 1 + h, 3 * h), z, core)

    def rank_peer(m):
        return device(x, 2 * y_hi + lax.rem(lax.div(m, 2), 2), lax.div(m, 4), lax.rem(m, 2))

    return p, r, slot_peer, rank_peer


def locate(plan_ref, block, nblocks):
    slot = jnp.int32(0)
    for j in range(nblocks):
        slot = jnp.where(plan_ref[1, j] == block, j, slot)
    return slot


def kernel(
    total_rows,
    plan_hbm,
    slab_ref,
    out_ref,
    vals_ref,
    recv_b,
    recv_s,
    plan_ref,
    xin,
    send_f,
    recv_f,
    part,
    gather_p,
    dpart,
    gather_d,
    gram,
    send_b,
    spart,
    gather_s,
    sfin,
    in_sem,
    f_send,
    f_recv,
    p_send,
    p_recv,
    d_send,
    d_recv,
    g_send,
    g_recv,
    b_send,
    b_recv,
    s_send,
    s_recv,
    v_send,
    v_recv,
):
    nrow, npair = lax.axis_size("row"), lax.axis_size("pair")
    row, pair = lax.axis_index("row"), lax.axis_index("pair")
    nblocks = 2 * npair
    rows, width = xin.shape[1:]
    half = width // LANE
    group = npair * rows
    if (nrow, npair) == (16, 8):
        p, r, slot_peer, rank_peer = torus_places(row, pair)
    else:
        p, r, slot_peer, rank_peer = ring_places(row, pair, nrow, npair)
    slots = [lax.rem(p + k, npair) for k in range(npair)]
    ranks = [lax.rem(r + k, nrow) for k in range(nrow)]
    if (nrow, npair) == (16, 8):
        far_first = (2, 1, 3, 0)
        slots = [
            lax.rem(lax.div(p, 4) + dy, 2) * 4 + lax.rem(p + dx, 4)
            for dx in far_first
            for dy in (1, 0)
            if dx or dy
        ]
        slots = [p] + slots
        ranks = [
            (lax.rem(lax.div(r, 4) + dz, 4) * 2 + lax.rem(lax.div(r, 2) + dy, 2)) * 2
            + lax.rem(r + dc, 2)
            for dz in far_first
            for dy in (1, 0)
            for dc in (1, 0)
            if dz or dy or dc
        ]
        ranks = [r] + ranks
    by_slot = [None] + [slot_peer(slot) for slot in slots[1:]]
    by_rank = [None] + [rank_peer(rank) for rank in ranks[1:]]
    others, peers = pl.ds(0, nrow - 1), pl.ds(0, npair - 1)

    def copy_to(device, src, dst, ssem, rsem):
        return pltpu.make_async_remote_copy(
            src_ref=src, dst_ref=dst, send_sem=ssem, recv_sem=rsem,
            device_id=device, device_id_type=MESH,
        )

    plan_load = pltpu.make_async_copy(plan_hbm, plan_ref, in_sem.at[0])
    plan_load.start()
    barrier = pltpu.get_barrier_semaphore()
    for device in by_slot[1:] + by_rank[1:]:
        pl.semaphore_signal(barrier, inc=1, device_id=device, device_id_type=MESH)
    for j in range(nblocks):
        pltpu.make_async_copy(
            slab_ref.at[:, j * width : (j + 1) * width], xin.at[j], in_sem.at[1]
        ).start()
    plan_load.wait()

    def origin(edge, side):
        keep = plan_ref[1, 2 * edge + side]
        other = jnp.int32(0)
        sign = jnp.float32(0.0)
        for j in range(0, nblocks, 2):
            first, second = plan_ref[0, j], plan_ref[0, j + 1]
            other = jnp.where(first == keep, second, other)
            sign = jnp.where(first == keep, -1.0, sign)
            other = jnp.where(second == keep, first, other)
            sign = jnp.where(second == keep, 1.0, sign)
        return keep, other, sign

    pltpu.make_async_copy(xin, xin, in_sem.at[1]).wait()
    signs = []
    for side in range(2):
        for k in range(1, npair):
            keep, other, _ = origin(slots[k], side)
            send_f[side, k - 1, :, :width] = xin[keep]
            send_f[side, k - 1, :, width:] = xin[other]
        if side == 0:
            pl.semaphore_wait(barrier, nrow + npair - 2)
        for k in range(1, npair):
            copy_to(
                by_slot[k], send_f.at[side, k - 1], recv_f.at[side, p], f_send,
                f_recv.at[side],
            ).start()
    for side in range(2):
        keep, other, sign = origin(p, side)
        signs.append(sign)
        recv_f[side, p, :, :width] = xin[keep]
        recv_f[side, p, :, width:] = xin[other]

    def wait_recv(ref, sem):
        copy_to(by_rank[1], ref, ref, sem, sem).wait_recv()

    def wait_send(ref, sem):
        copy_to(by_rank[1], ref, ref, sem, sem).wait_send()

    def reduce_start(n, first, second):
        turned, right = first.T, split(second)
        band, span = width // BANDS, width // HALVES
        for g in range(BANDS):
            left = split(turned[g * band : (g + 1) * band])
            product = dot3(left, right)
            for c in range(HALVES):
                h = g * HALVES + c
                part[n, h] = product[:, c * span : (c + 1) * span].reshape(
                    part.shape[2:]
                )
                for k in range(1, nrow):
                    copy_to(
                        by_rank[k], part.at[n, h, ranks[k]], gather_p.at[n, h, r],
                        p_send, p_recv.at[n, h],
                    ).start()
        for h in range(CHUNKS):
            gather_p[n, h, r] = part[n, h, r]

    def squares_start(n, first, second):
        sums = jnp.concatenate(
            [
                jnp.sum(first * first, axis=0, keepdims=True),
                jnp.sum(second * second, axis=0, keepdims=True),
            ],
            axis=1,
        )
        for i in range(2 * half):
            dpart[n, i : i + 1, :] = sums[:, i * LANE : (i + 1) * LANE]
        for k in range(1, nrow):
            copy_to(
                by_rank[k], dpart.at[n], gather_d.at[n, r], d_send, d_recv.at[n]
            ).start()
        gather_d[n, r] = dpart[n]

    def reduce_middle(n):
        for h in range(CHUNKS):
            wait_recv(gather_p.at[n, h, others], p_recv.at[n, h])
            total = gather_p[n, h, 0]
            for j in range(1, nrow):
                total = total + gather_p[n, h, j]
            gram[n, h, r] = total
            for k in range(1, nrow):
                copy_to(
                    by_rank[k], gram.at[n, h, r], gram.at[n, h, r], g_send, g_recv.at[n]
                ).start()

    def denominator(n):
        wait_recv(gather_d.at[n, others], d_recv.at[n])
        sums = gather_d[n, 0]
        for j in range(1, nrow):
            sums = sums + gather_d[n, j]
        return column(sums, 0, width) + (line(sums, half, width) + 1e-6)

    def reduced(n):
        wait_recv(gram.at[n, :, others], g_recv.at[n])
        return jnp.concatenate(
            [
                jnp.concatenate(
                    [
                        gram[n, g * HALVES + c].reshape(width // BANDS, -1)
                        for c in range(HALVES)
                    ],
                    axis=1,
                )
                for g in range(BANDS)
            ],
            axis=0,
        )

    ident = (
        lax.broadcasted_iota(jnp.int32, (width, width), 0)
        == lax.broadcasted_iota(jnp.int32, (width, width), 1)
    ).astype(jnp.float32)

    def begin(couple, keep, other, sign):
        pieces = split(couple)
        scale = 1.0 + jnp.sum(couple * couple, keepdims=True)
        inv = 1.0 / scale
        inner = (ident + dot3(pieces, pieces, ROWS_BY_ROWS)) * inv
        mixed = keep + sign * dot3(split(other), pieces, ROWS_BY_ROWS)
        return inner, mixed * (0.5 * jnp.sqrt(inv))

    def factors_of(inner):
        product = None
        for step in range(NS_STEPS):
            factor = 1.5 * ident - 0.5 * inner
            fs = split(factor)
            product = 2.0 * factor if step == 0 else dot3(split(product), fs)
            if step + 1 < NS_STEPS:
                inner = dot3(split(dot3(split(inner), fs)), fs)
        return split(product)

    def rotate(items):
        inners, outs = [], []
        for item in items:
            inner, out = begin(*item)
            inners.append(inner)
            outs.append(2.0 * out)
        for step in range(NS_STEPS):
            factors = [split(1.5 * ident - 0.5 * inner) for inner in inners]
            if step + 1 == NS_STEPS:
                return [
                    functools.partial(dot3, split(out), fs)
                    for out, fs in zip(outs, factors)
                ]
            inners = [dot3(split(inner), fs) for inner, fs in zip(inners, factors)]
            outs = [dot3(split(out), fs) for out, fs in zip(outs, factors)]
            inners = [dot3(split(inner), fs) for inner, fs in zip(inners, factors)]

    wait_recv(recv_f.at[0, peers], f_recv.at[0])
    both = recv_f[0].reshape(group, 2 * width)
    reduce_start(0, both[:, :width], both[:, width:])
    both = recv_f[0].reshape(group, 2 * width)
    squares_start(0, both[:, :width], both[:, width:])
    wait_recv(recv_f.at[1, peers], f_recv.at[1])
    both = recv_f[1].reshape(group, 2 * width)
    reduce_start(1, both[:, :width], both[:, width:])
    both = recv_f[1].reshape(group, 2 * width)
    squares_start(1, both[:, :width], both[:, width:])
    reduce_middle(0)
    reduce_middle(1)
    denoms = [denominator(side) for side in range(2)]

    mixes, turns = [], []
    for side in range(2):
        couple = reduced(side) / denoms[side]
        both = recv_f[side].reshape(group, 2 * width)
        inner, mixed = begin(couple, both[:, :width], both[:, width:], signs[side])
        mixes.append(mixed)
        if side == 1:
            reduce_start(2, *mixes)
        turns.append(factors_of(inner))

    blocks = [dot3(split(mixed), turn) for mixed, turn in zip(mixes, turns)]
    squares_start(2, *blocks)
    reduce_middle(2)
    denom = denominator(2)
    middle = dot3(split(reduced(2)), turns[1])
    couple = dot3(turns[0], split(middle)) / denom
    lasts = rotate(
        [(couple, *blocks, -1.0), (couple.T, blocks[1], blocks[0], 1.0)]
    )
    for side in range(2):
        final = lasts[side]()
        send_b[side] = final.reshape(npair, rows, width)
        for k in range(1, npair):
            copy_to(
                by_slot[k], send_b.at[side, slots[k]], recv_b.at[2 * p + side], b_send,
                b_recv,
            ).start()
        sums = jnp.sum(final * final, axis=0, keepdims=True)
        for i in range(half):
            spart[side * half + i : side * half + i + 1, :] = sums[
                :, i * LANE : (i + 1) * LANE
            ]
    for k in range(1, nrow):
        copy_to(by_rank[k], spart, gather_s.at[r], s_send, s_recv).start()
    gather_s[r] = spart[...]
    mine = pl.ds(2 * p, 2)
    for side in range(2):
        recv_b[2 * p + side] = send_b[side, p]

    wait_recv(gather_s.at[others], s_recv)
    sums = gather_s[0]
    for j in range(1, nrow):
        sums = sums + gather_s[j]
    vals = jnp.sqrt(sums / total_rows)
    for side in range(2):
        sfin[side] = vals[side * half : (side + 1) * half]
    for k in range(1, npair):
        copy_to(by_slot[k], sfin, recv_s.at[mine], v_send, v_recv).start()
    recv_s[mine] = sfin[...]

    arrived = pl.ds(0, 2 * (npair - 1))
    wait_send(send_f.at[:, peers], f_send)
    wait_send(gather_d.at[:, others], d_send)
    wait_send(gather_p.at[:, :, others], p_send)
    wait_send(gram.at[:, :, others], g_send)
    wait_send(gather_s.at[others], s_send)
    wait_send(send_b.at[:, peers], b_send)
    wait_send(recv_s.at[arrived], v_send)
    wait_recv(recv_b.at[arrived], b_recv)
    wait_recv(recv_s.at[arrived], v_recv)
    for j in range(nblocks):
        slot = locate(plan_ref, j, nblocks)
        out_ref[:, j * width : (j + 1) * width] = recv_b[slot]
        vals_ref[j * half : (j + 1) * half, :] = recv_s[slot]


def solution(mesh):
    nrow, npair = mesh.shape["row"], mesh.shape["pair"]
    vmem, smem = pltpu.VMEM, pltpu.SMEM
    anywhere = pl.BlockSpec(memory_space=pl.ANY)

    def on_device(slab, plan):
        rows, ncols = slab.shape
        nblocks = 2 * npair
        width = ncols // nblocks
        part_rows = width // (nrow * BANDS)
        half = width // LANE
        f32 = jnp.float32
        dma = pltpu.SemaphoreType.DMA
        out, vals = pl.pallas_call(
            functools.partial(kernel, rows * nrow * npair),
            out_shape=(
                pltpu.VMEM((rows, ncols), f32),
                pltpu.VMEM((nblocks * half, LANE), f32),
            ),
            in_specs=[anywhere, anywhere],
            out_specs=(pl.BlockSpec(memory_space=vmem), pl.BlockSpec(memory_space=vmem)),
            scratch_shapes=[
                vmem((nblocks, rows, width), f32),
                vmem((nblocks, half, LANE), f32),
                smem(plan.shape, jnp.int32),
                vmem((nblocks, rows, width), f32),
                vmem((2, npair - 1, rows, 2 * width), f32),
                vmem((2, npair, rows, 2 * width), f32),
                vmem((3, CHUNKS, nrow, part_rows, width // HALVES), f32),
                vmem((3, CHUNKS, nrow, part_rows, width // HALVES), f32),
                vmem((3, 2 * half, LANE), f32),
                vmem((3, nrow, 2 * half, LANE), f32),
                vmem((3, CHUNKS, nrow, part_rows, width // HALVES), f32),
                vmem((2, npair, rows, width), f32),
                vmem((2 * half, LANE), f32),
                vmem((nrow, 2 * half, LANE), f32),
                vmem((2, half, LANE), f32),
                dma((2,)),
                dma,
                dma((2,)),
                dma,
                dma((3, CHUNKS)),
                dma,
                dma((3,)),
                dma,
                dma((3,)),
                dma,
                dma,
                dma,
                dma,
                dma,
                dma,
            ],
            compiler_params=pltpu.CompilerParams(
                collective_id=0, has_side_effects=True, vmem_limit_bytes=66000000
            ),
        )(plan, slab)
        return out, vals.reshape(ncols)

    return jax.shard_map(
        on_device,
        mesh=mesh,
        in_specs=(P(("row", "pair"), None), P()),
        out_specs=(P(("row", "pair"), None), P()),
        check_vma=False,
    )
```
